32 devices in a mesh: sub: 8 (over z, x), col: 4 (over y, core).
Axes of the slice: x: 2, y: 2, z: 4, core: 2. Of those that a mesh axis runs over, the one named last changes fastest.
Arguments:
- adjoint_source: float32 [64, 12288], P('col', 'sub'), may hold values from -4 to 4
- start_field: float32 [64, 12288], P('col', 'sub'), may hold values from -3 to 3
- row_diagonal: float32 [12288], P('sub'), may hold values from 2 to 4
- row_values: float32 [26, 12288], P(None, 'sub'), may hold values from -0.6 to 0.6
- row_columns: int32 [26, 12288], P(None, 'sub'), may hold values from 0 to 2047
- weight_code: int32 [16384], P('sub'), may hold values from 0 to 3
- slot_count: int32 [8, 4], P('sub'), may hold values from 0 to 128, as said below
- slot_rows: int32 [8, 4, 128], P('sub'), may hold values from 0 to 1535, as said below
- local_inverse: float32 [16384, 2048], P(('sub', 'col')), may hold values from -0.006629126 to 0.60662913
- coarse_modes: float32 [4, 12288], P(None, 'sub'), may hold values from -0.15309311 to 0.15309311
- coarse_inverse: float32 [32, 32], P('sub'), may hold values from -0.079549513 to 0.6795495
Outputs:
- adjoint: float32 [64, 12288], P('col', 'sub')
The draws below stay inside these ranges and needn't reach their ends.
Inputs may be any that keep to these rules, and one draw needn't show every extreme that they name: slot_count[s, d] counts the live slots that subdomain s takes from subdomain s - 2, s - 1, s + 1, s + 2 for d = 0, 1, 2, 3; it is zero where that subdomain does not exist, and some entry equals 128 in every draw. `slot_rows`: the entries of one subdomain and direction are distinct.
All inputs are finite; a program needn't handle non-finite values.
Results may differ from the reference program's by a relative error of at most 0.00016.
Values sent between devices are 32-bit elements; how exact they have to be, the bound alone decides.
A program may use at most 128 MiB of HBM per device.

```python
import math
import jax
import jax.numpy as jnp
from jax import lax

OWN = 1536
MAXR = 128
TERMS = 26
MODES = 4
ITERS = 3
EXT = 2048
SUBS = 8
NCOL = 64
NTOT = 12288
NEXT = 16384
COARSE = 32


def draw_adjoint_source(key, part):
    return jnp.clip(jax.random.normal(key, (NCOL, NTOT), jnp.float32), -4.0, 4.0)


def inverse_draw(key, blocks, order, off_scale):
    key_diag, key_off = jax.random.split(jax.random.fold_in(key, 11))
    half_width = off_scale / order ** 0.5
    spread = jax.random.uniform(key_off, (blocks * order, order), jnp.float32, -half_width, half_width)
    diagonal = jnp.exp(jax.random.uniform(key_diag, (blocks * order,), jnp.float32, math.log(0.3), math.log(0.6)))
    row_index = jnp.arange(blocks * order, dtype=jnp.int32) % order
    column_index = jnp.arange(order, dtype=jnp.int32)
    return spread + jnp.where(row_index[:, None] == column_index[None, :], diagonal[:, None], 0.0)


def draw_local_inverse(key, part):
    return inverse_draw(key, SUBS, EXT, 0.3)


def draw_coarse_inverse(key, part):
    return inverse_draw(key, 1, COARSE, 0.45)


def draw_slot_count(key, part):
    key_one, key_two, key_three = jax.random.split(jax.random.fold_in(key, 23), 3)
    source = jnp.arange(SUBS, dtype=jnp.int32)[:, None] + jnp.array([-2, -1, 1, 2], dtype=jnp.int32)[None, :]
    inside = (source >= 0) & (source < SUBS)
    amount = jax.random.randint(key_one, (SUBS, 4), MAXR // 4, MAXR + 1)
    present = jax.random.randint(key_two, (SUBS, 4), 0, 2)
    far_mask = jnp.array([1, 0, 0, 1], dtype=jnp.int32)[None, :]
    amount = amount * jnp.where(far_mask == 1, present, 1)
    amount = jnp.where(inside, amount, 0)
    chosen = jax.random.randint(key_three, (), 0, SUBS - 1)
    amount = amount.at[chosen, 2].set(MAXR)
    return amount.astype(jnp.int32)


def draw_slot_rows(key, part):
    subkeys = jax.random.split(jax.random.fold_in(key, 31), SUBS * 4)

    def one_list(single):
        return jax.random.permutation(single, OWN)[:MAXR]
    picked = jax.vmap(one_list)(subkeys)
    return picked.reshape(SUBS, 4, MAXR).astype(jnp.int32)


def with_ends(entries, rng, low, high):
    longest = entries.shape.index(max(entries.shape))
    spots = []
    for shift in (0, 1):
        where = [jax.random.randint(jax.random.fold_in(rng, axis), (), 0, length) for axis, length in enumerate(entries.shape)]
        where[longest] = (where[longest] + shift) % entries.shape[longest]
        spots.append(tuple(where))
    return entries.at[spots[0]].set(low).at[spots[1]].set(high)


def levels(stream_key, shape, cuts, least, top_value):
    loudness, own = 1.0, jax.random.fold_in(stream_key, 6)
    for position, blocks in cuts:
        draws = jnp.exp(jax.random.uniform(jax.random.fold_in(own, position), (blocks,), jnp.float32, least / len(cuts), top_value / len(cuts)))
        loudness = loudness * jnp.repeat(draws, shape[position] // blocks).reshape([-1 if axis == position else 1 for axis in range(len(shape))])
    return loudness


def centred(stream_key, extent, deviation, bound, shards=(), held_as=jnp.bfloat16):
    drawn = jax.random.normal(stream_key, extent, jnp.float32) * deviation
    if len(shards) > 0:
        drawn = levels(stream_key, extent, shards, -0.22, 0.18) * drawn
    return jnp.clip(drawn, min=-bound, max=bound).astype(held_as)


def setup_inputs(seed: int = 0) -> dict:
    key_list = jax.random.split(jax.random.key(seed), 12)
    adjoint_source = draw_adjoint_source(jax.random.fold_in(key_list[11], 71), 0)
    start_field = centred(key_list[1], (NCOL, NTOT), 0.5, 3.0, ((0, 4), (1, 8)), jnp.float32)
    row_diagonal = jnp.clip(jnp.exp(math.log(4.0) - 0.6931472 * jax.random.uniform(key_list[2], (NTOT,), jnp.float32) ** levels(key_list[2], (NTOT,), ((0, 8),), -0.2, 0.2)), 2.0, 4.0)
    row_values = centred(key_list[3], (TERMS, NTOT), 0.15, 0.6, ((1, 8),), jnp.float32)
    row_columns = with_ends(jax.random.randint(key_list[4], (TERMS, NTOT), 0, EXT), jax.random.fold_in(key_list[4], 1), 0, EXT - 1).astype(jnp.int32)
    weight_code = with_ends(jax.random.randint(key_list[5], (NEXT,), 0, 4), jax.random.fold_in(key_list[5], 1), 0, 3).astype(jnp.int32)
    slot_count = draw_slot_count(jax.random.fold_in(key_list[11], 71), 0)
    slot_rows = draw_slot_rows(jax.random.fold_in(key_list[11], 71), 0)
    local_inverse = draw_local_inverse(jax.random.fold_in(key_list[11], 71), 0)
    coarse_modes = centred(key_list[9], (MODES, NTOT), (1.3 / OWN ** 0.5), 0.15309311, ((1, 8),), jnp.float32)
    coarse_inverse = draw_coarse_inverse(jax.random.fold_in(key_list[11], 71), 0)
    return dict(adjoint_source=adjoint_source, start_field=start_field, row_diagonal=row_diagonal, row_values=row_values, row_columns=row_columns, weight_code=weight_code, slot_count=slot_count, slot_rows=slot_rows, local_inverse=local_inverse, coarse_modes=coarse_modes, coarse_inverse=coarse_inverse)


direction_steps = (-2, -1, 1, 2)
damping = 0.7
highest = lax.Precision.HIGHEST


def extend(values, slot_count, slot_rows):
    index_list = jnp.arange(SUBS, dtype=jnp.int32)
    slot_index = jnp.arange(MAXR, dtype=jnp.int32)
    pieces = [values]
    for number, offset in enumerate(direction_steps):
        source = jnp.clip(index_list + offset, 0, SUBS - 1)
        shifted = values[:, source, :]
        wanted = jnp.broadcast_to(slot_rows[None, :, number, :], (values.shape[0], SUBS, MAXR))
        taken_rows = jnp.take_along_axis(shifted, wanted, axis=2)
        live_mask = (slot_index[None, :] < slot_count[:, number:number + 1]).astype(values.dtype)
        pieces.append(taken_rows * live_mask[None])
    return jnp.concatenate(pieces, axis=2)


def reference(adjoint_source, start_field, row_diagonal, row_values, row_columns, weight_code, slot_count, slot_rows, local_inverse, coarse_modes, coarse_inverse):
    columns = adjoint_source.shape[0]
    source_grid = adjoint_source.reshape(columns, SUBS, OWN)
    field_grid = start_field.reshape(columns, SUBS, OWN)
    diagonal_grid = row_diagonal.reshape(SUBS, OWN)
    values_grid = row_values.reshape(TERMS, SUBS, OWN)
    indices_grid = row_columns.reshape(TERMS, SUBS, OWN)
    weights = 1.0 / (1.0 + weight_code.reshape(SUBS, EXT).astype(jnp.float32))
    inverse_grid = local_inverse.reshape(SUBS, EXT, EXT)
    modes_grid = coarse_modes.reshape(MODES, SUBS, OWN)
    slot_index = jnp.arange(MAXR, dtype=jnp.int32)
    index_list = jnp.arange(SUBS, dtype=jnp.int32)

    def solve_one(operands):
        block_inverse, block_rhs = operands
        return lax.dot_general(block_rhs, block_inverse, (((1,), (1,)), ((), ())), precision=highest)

    for iteration in range(ITERS):
        extended = extend(field_grid, slot_count, slot_rows)

        def add_term(running, term_pair):
            term_values, term_columns = term_pair
            wanted = jnp.broadcast_to(term_columns[None], running.shape)
            taken_rows = jnp.take_along_axis(extended, wanted, axis=2)
            return running + term_values[None] * taken_rows, None

        residual_sum, unused = lax.scan(add_term, jnp.zeros_like(field_grid), (values_grid, indices_grid))
        residual = source_grid - diagonal_grid[None] * field_grid - residual_sum
        weighted = extend(residual, slot_count, slot_rows) * weights[None]
        solved = lax.map(solve_one, (inverse_grid, jnp.transpose(weighted, (1, 0, 2))))
        solved = jnp.transpose(solved, (1, 0, 2))
        correction = solved[:, :, :OWN]
        for number, offset in enumerate(direction_steps):
            live_mask = (slot_index[None, :] < slot_count[:, number:number + 1]).astype(field_grid.dtype)
            slot_values = solved[:, :, OWN + number * MAXR:OWN + (number + 1) * MAXR] * live_mask[None]
            target = jnp.broadcast_to(jnp.clip(index_list + offset, 0, SUBS - 1)[:, None], (SUBS, MAXR))
            correction = correction.at[:, target, slot_rows[:, number, :]].add(slot_values)
        coarse_rhs = jnp.einsum("csi,msi->csm", residual, modes_grid, precision=highest).reshape(columns, COARSE)
        coarse = lax.dot_general(coarse_rhs, coarse_inverse, (((1,), (1,)), ((), ())), precision=highest)
        coarse = coarse.reshape(columns, SUBS, MODES)
        lifted = jnp.einsum("csm,msi->csi", coarse, modes_grid, precision=highest)
        field_grid = field_grid + damping * (correction + lifted)
    return field_grid.reshape(columns, SUBS * OWN)
```

```python
import functools

import jax
import jax.numpy as jnp
from jax import lax
from jax.experimental import pallas as pl
from jax.experimental.pallas import tpu as pltpu
from jax.sharding import PartitionSpec as P

ITERS = 3
LANES = 128
SUBLANES = 8

direction_steps = (-2, -1, 1, 2)
damping = 0.7
highest = lax.Precision.HIGHEST
contract_last = (((1,), (1,)), ((), ()))
contract_first = (((1,), (0,)), ((), ()))
f32 = jnp.float32
bf16 = jnp.bfloat16
DIRS = len(direction_steps)
GROUPS = 1


def lane_gather(tile, low):
    return jnp.take_along_axis(tile, low, axis=1, mode="promise_in_bounds")


def split(x):
    high = x.astype(bf16)
    return high, (x - high.astype(f32)).astype(bf16)


def build_operator(idx_ref, vals_ref, op_hi, op_lo, turned, low_rows):
    terms, owned = idx_ref.shape
    heads = op_hi.shape[0] // LANES
    tiles = owned // LANES
    width = 1 << (terms - 1).bit_length()
    per = LANES // width
    halves = SUBLANES // per
    blocks = LANES // SUBLANES
    full = (LANES, LANES)
    square_row = lax.broadcasted_iota(jnp.int32, full, 0)
    square_lane = lax.broadcasted_iota(jnp.int32, full, 1)
    eye = jnp.where(square_row == square_lane, 1.0, 0.0).astype(bf16)
    keep = [square_row % SUBLANES == square_lane // width + per * h for h in range(halves)]
    few = (blocks, LANES)
    pick = lax.broadcasted_iota(jnp.int32, few, 1) // SUBLANES == lax.broadcasted_iota(jnp.int32, few, 0)
    pick = jnp.where(pick, 1.0, 0.0).astype(bf16)

    def turn(t, carry):
        at = pl.ds(pl.multiple_of(t * LANES, LANES), LANES)
        index, value = idx_ref[:, at], vals_ref[:, at]

        def tiled(x, fill):
            x = jnp.concatenate([x, jnp.full((width - terms, LANES), fill, f32)], axis=0)
            return jnp.concatenate([x] * per, axis=0).astype(bf16)

        def turn_one(x):
            return lax.dot_general(eye, x, contract_last, preferred_element_type=f32)

        top = value.astype(bf16).astype(f32)
        turned[0, at, :] = turn_one(tiled((index >> 7).astype(f32), -1.0))
        turned[1, at, :] = turn_one(tiled(top, 0.0))
        turned[2, at, :] = turn_one(tiled(value - top, 0.0))
        low = turn_one(tiled((index & (LANES - 1)).astype(f32), -1.0))
        for h in range(halves):
            low_rows[h, pl.ds(pl.multiple_of(t * blocks, blocks), blocks), :] = lax.dot_general(
                pick, jnp.where(keep[h], low, 0.0).astype(bf16), contract_first, preferred_element_type=f32
            )
        return carry

    lax.fori_loop(0, tiles, turn, 0, unroll=tiles)

    lane_number = square_row.astype(f32).astype(bf16)
    tall = (heads * SUBLANES, LANES)
    head_number = (lax.broadcasted_iota(jnp.int32, tall, 0) // SUBLANES).astype(f32).astype(bf16)
    small = (SUBLANES, LANES)
    mine = [
        lax.broadcasted_iota(jnp.int32, small, 0) == lax.broadcasted_iota(jnp.int32, small, 1) // width + per * h
        for h in range(halves)
    ]
    one, zero = jnp.ones(full, bf16), jnp.zeros(full, bf16)
    none = jnp.zeros(tall, bf16)

    def repeat(x):
        pair = jnp.concatenate([x, x], axis=0).astype(bf16)
        return jnp.concatenate([pair] * (heads // 2), axis=0)

    def one_block(row):
        at = pl.ds(pl.multiple_of(row * SUBLANES, SUBLANES), SUBLANES)
        head = turned[0, at, :]
        value_hi, value_lo = repeat(turned[1, at, :]), repeat(turned[2, at, :])
        left_hi, left_lo, right = [], [], []
        for h in range(halves):
            hit = repeat(jnp.where(mine[h], head, -1.0)) == head_number
            left_hi.append(jnp.where(hit, value_hi, none))
            left_lo.append(jnp.where(hit, value_lo, none))
            low = jnp.broadcast_to(low_rows[h, pl.ds(row, 1), :], (2 * SUBLANES, LANES)).astype(bf16)
            low = jnp.concatenate([low] * (LANES // (2 * SUBLANES)), axis=0)
            right.append(jnp.where(low == lane_number, one, zero))
        left = jnp.concatenate([jnp.concatenate(left_hi, axis=1), jnp.concatenate(left_lo, axis=1)], axis=0)
        out = lax.dot_general(left, jnp.concatenate(right, axis=1), contract_last, preferred_element_type=f32)
        return out[: heads * SUBLANES] + out[heads * SUBLANES :]

    def one_tile(t, carry):
        at = pl.ds(pl.multiple_of(t * LANES, LANES), LANES)
        outs = [one_block(t * blocks + b) for b in range(blocks)]
        for h in range(heads):
            x = jnp.concatenate([out[h * SUBLANES : (h + 1) * SUBLANES] for out in outs], axis=0).T
            high, low = split(x)
            op_hi[h * LANES : (h + 1) * LANES, at] = high
            op_lo[h * LANES : (h + 1) * LANES, at] = low
        return carry

    lax.fori_loop(0, tiles, one_tile, 0, unroll=2)


def kernel(
    subs, cols,
    source_ref, start_ref, diag_ref, vals_ref, idx_ref, code_ref, count_ref, rows_ref, modes_ref, cinv_ref, li_hbm,
    out_ref,
    lam, base, op_hi, op_lo, turned, low_rows, li, li_hi, li_lo, table, tables, fidx, inverse, cinv_pad, cinv_turned,
    halo_out, halo_in, own_x, mar_out, mar_x, coarse_x, solved, sol_in, ret_in,
    li_sem, tab_s, tab_r, halo_s, halo_r, own_s, own_r, mar_s, mar_r, co_s, co_r, sol_s, sol_r, ret_s, ret_r,
):
    s = lax.axis_index("sub")
    c = lax.axis_index("col")
    owned = start_ref.shape[1]
    rows = lam.shape[1]
    tiles = owned // LANES
    early = tiles // 2
    block = li_hbm.shape[0]
    nmodes = modes_ref.shape[0]
    cuts = ((0, early * LANES), (early * LANES, owned - early * LANES))

    def sub_at(by):
        return lax.rem(s + (by + subs), subs)

    def col_at(by):
        return lax.rem(c + (by + cols), cols)

    def inside(by):
        return jnp.logical_and(s + by >= 0, s + by < subs)

    def remote(src, dst, send, recv, where):
        return pltpu.make_async_remote_copy(
            src_ref=src, dst_ref=dst, send_sem=send, recv_sem=recv,
            device_id=where, device_id_type=pl.DeviceIdType.MESH,
        )

    load_inverse = pltpu.make_async_copy(li_hbm, li, li_sem)
    load_inverse.start()

    partners = []
    for step in range(1, cols):
        partners.append((0, step))
    for by in range(1, subs):
        near = by in (1, 2, subs - 1, subs - 2)
        for step in range(cols if near else 1):
            partners.append((by, step))
    barrier = pltpu.get_barrier_semaphore()
    tables[...] = jnp.full(tables.shape, -1, jnp.int32)
    for clean in (halo_in, mar_x, ret_in, coarse_x):
        clean[...] = jnp.zeros_like(clean)
    for by, step in partners:
        pl.semaphore_signal(
            barrier, inc=1, device_id=(sub_at(by), col_at(step)), device_id_type=pl.DeviceIdType.MESH
        )
    lane = lax.broadcasted_iota(jnp.int32, (1, LANES), 1)
    for d in range(DIRS):
        table[pl.ds(d, 1), :] = jnp.where(lane < count_ref[0, d], rows_ref[0, pl.ds(d, 1), :], -1)
    for g in range(GROUPS):
        lam[g] = start_ref[g * rows : (g + 1) * rows, :]
    members = subs * nmodes
    cinv_pad[...] = jnp.zeros_like(cinv_pad)
    cinv_pad[pl.ds(0, nmodes), :] = cinv_ref[...]
    square = (members, members)
    same = lax.broadcasted_iota(jnp.int32, square, 0) == lax.broadcasted_iota(jnp.int32, square, 1)
    cinv_turned[...] = lax.dot_general(
        jnp.where(same, 1.0, 0.0), cinv_pad[...], contract_last, precision=highest, preferred_element_type=f32
    )

    pl.semaphore_wait(barrier, len(partners))

    def tab_copy(d):
        return remote(table, tables.at[d], tab_s.at[d], tab_r.at[d], (sub_at(direction_steps[d]), c))

    for d in range(DIRS):

        @pl.when(inside(direction_steps[d]))
        def _():
            tab_copy(d).start()

    def read_tables():
        for d in range(DIRS):

            @pl.when(inside(direction_steps[d]))
            def _():
                tab_copy(d).wait_send()

            @pl.when(inside(-direction_steps[d]))
            def _():
                tab_copy(d).wait_recv()

        for d in range(DIRS):
            fidx[pl.ds(d, 1), :] = tables[d, pl.ds(d, 1), :]

        slot_number = lax.broadcasted_iota(jnp.int32, (LANES, LANES), 0).astype(f32) + 1.0
        lane_full = lax.broadcasted_iota(jnp.int32, (LANES, LANES), 1).astype(f32)
        for d in range(DIRS):
            wanted = jnp.broadcast_to(fidx[pl.ds(d, 1), :].astype(f32), (LANES, LANES)).T

            def invert(number, carry):
                hit = wanted == lane_full + lax.convert_element_type(number * LANES, f32)
                found = jnp.sum(jnp.where(hit, slot_number, 0.0), axis=0, keepdims=True)
                inverse[number, pl.ds(d, 1), :] = found.astype(jnp.int32) - 1
                return carry

            lax.fori_loop(0, tiles, invert, 0)

    def pack(read_tile, put):
        for d in range(DIRS):
            index = jnp.broadcast_to(fidx[pl.ds(d, 1), :], (rows, LANES))
            low, high = index & (LANES - 1), index >> 7
            total = jnp.zeros((rows, LANES), f32)
            for t in range(tiles):
                total = jnp.where(high == t, lane_gather(read_tile(t), low), total)
            put(d, total)

    def operate(x, low, high, at):
        count = x.shape[0]
        top, bottom = split(x)
        stretch = pl.ds(low, high - low)
        both = jnp.dot(jnp.concatenate([top, bottom], axis=0), op_hi[stretch, at], preferred_element_type=f32)
        cross = jnp.dot(top, op_lo[stretch, at], preferred_element_type=f32)
        return both[:count] + (both[count:] + cross)

    own_parts = [max(0, min((b + 1) * block, owned) - b * block) for b in range(cols)]
    slot_homes = [divmod(owned + d * LANES, block) for d in range(DIRS)]

    def halo_copy(q, d):
        return remote(
            halo_out.at[q, d], halo_in.at[q, d], halo_s.at[q, d], halo_r.at[q, d], (sub_at(-direction_steps[d]), c)
        )

    def own_copy(q, part, step, slot):
        piece = own_x.at[q, slot, :, pl.ds(*cuts[part])]
        return remote(piece, piece, own_s.at[q, part, step], own_r.at[q, part, step], (s, col_at(step)))

    def mar_copy(q, d, step, slot):
        return remote(
            mar_out.at[q, d], mar_x.at[q, d, slot], mar_s.at[q, d, step], mar_r.at[q, d, step],
            (sub_at(-direction_steps[d]), col_at(step)),
        )

    def coarse_copy(q, by, slot):
        return remote(coarse_x.at[q, slot], coarse_x.at[q, slot], co_s.at[q, by], co_r.at[q, by], (sub_at(by), c))

    def sol_copy(q, b, step):
        width = own_parts[b]
        return remote(
            solved.at[q, col_at(step), :, pl.ds(0, width)], sol_in.at[q, b, :, pl.ds(0, width)],
            sol_s.at[q, step], sol_r.at[q, b], (s, col_at(step)),
        )

    def ret_copy(q, d, step):
        return remote(
            solved.at[q, col_at(step), :, pl.ds(slot_homes[d][1], LANES)], ret_in.at[q, d],
            ret_s.at[q, d, step], ret_r.at[q, d], (sub_at(direction_steps[d]), col_at(step)),
        )

    def each_return(act):
        for d in range(DIRS):

            @pl.when(jnp.logical_and(c == slot_homes[d][0], inside(direction_steps[d])))
            def _():
                for step in range(cols):
                    act(d, step)

    def halos(g, q):
        def put_halo(d, total):
            halo_out[q, d] = total

            @pl.when(inside(-direction_steps[d]))
            def _():
                halo_copy(q, d).start()

        pack(lambda t: lam[g, :, t * LANES : (t + 1) * LANES], put_halo)

    def begin(g, q):
        for low, count in cuts:
            at = pl.ds(low, count)
            held = lam[g, :, at]
            base[:, at] = source_ref[g * rows : (g + 1) * rows, at] - diag_ref[:, at] * held - operate(lam[g], 0, owned, at)

    def rest(g, q):
        for d in range(DIRS):

            @pl.when(inside(direction_steps[d]))
            def _():
                halo_copy(q, d).wait_recv()

        slots = jnp.concatenate([halo_in[q, d] for d in range(DIRS)], axis=1)
        for part, (low, count) in enumerate(cuts):
            at = pl.ds(low, count)
            own_x[q, c, :, at] = base[:, at] - operate(slots, owned, owned + DIRS * LANES, at)
            for step in range(1, cols):
                own_copy(q, part, step, c).start()

        def put_margin(d, total):
            mar_out[q, d] = total

            @pl.when(inside(-direction_steps[d]))
            def _():
                for step in range(cols):
                    mar_copy(q, d, step, c).start()

        pack(lambda t: own_x[q, c, :, t * LANES : (t + 1) * LANES], put_margin)
        message = jnp.zeros((rows, LANES), f32)
        for m in range(nmodes):
            part = jnp.zeros((rows, LANES), f32)
            for t in range(tiles):
                at = pl.ds(t * LANES, LANES)
                part = part + own_x[q, c, :, at] * modes_ref[pl.ds(m, 1), at]
            message = jnp.where(lane == m, jnp.sum(part, axis=1, keepdims=True), message)
        coarse_x[q, s] = message
        for by in range(1, subs):
            coarse_copy(q, by, s).start()

    def product(x, at):
        high, low = split(x)
        count = x.shape[0]
        both = lax.dot_general(
            jnp.concatenate([high, low], axis=0), li_hi[:, at], contract_last, preferred_element_type=f32
        )
        cross = lax.dot_general(high, li_lo[:, at], contract_last, preferred_element_type=f32)
        return both[:count] + (both[count:] + cross)

    def solve(q):
        for part in range(len(cuts)):
            for step in range(1, cols):
                own_copy(q, part, step, col_at(-step)).wait_recv()
        total = product(own_x[q].reshape(cols * rows, owned), pl.ds(0, owned))
        for d in range(DIRS):

            @pl.when(inside(direction_steps[d]))
            def _():
                for step in range(cols):
                    mar_copy(q, d, step, col_at(-step)).wait_recv()

        margins = jnp.concatenate([mar_x[q, d].reshape(cols * rows, LANES) for d in range(DIRS)], axis=1)
        total = total + product(margins, pl.ds(owned, DIRS * LANES))
        solved[q] = total.reshape(cols, rows, block)
        each_return(lambda d, step: ret_copy(q, d, step).start())
        for b in range(cols):
            if own_parts[b]:

                @pl.when(c == b)
                def _():
                    for step in range(1, cols):
                        sol_copy(q, b, step).start()
                    sol_in[q, b, :, pl.ds(0, own_parts[b])] = solved[q, c, :, pl.ds(0, own_parts[b])]

    def update(g, q):
        for by in range(1, subs):
            coarse_copy(q, by, sub_at(-by)).wait_recv()
        coarse = jnp.zeros((rows, LANES), f32)
        for other in range(subs):
            message = coarse_x[q, other]
            for m in range(nmodes):
                coarse = coarse + message[:, m : m + 1] * cinv_turned[pl.ds(other * nmodes + m, 1), :]
        levels = [jnp.broadcast_to(coarse[:, m : m + 1], (rows, LANES)) for m in range(nmodes)]
        for b in range(cols):
            if own_parts[b]:

                @pl.when(c != b)
                def _():
                    sol_copy(q, b, 0).wait_recv()

        for d in range(DIRS):

            @pl.when(inside(-direction_steps[d]))
            def _():
                ret_copy(q, d, 0).wait_recv()

        for t in range(tiles):
            at = pl.ds(t * LANES, LANES)
            b, offset = divmod(t * LANES, block)
            total = sol_in[q, b, :, pl.ds(offset, LANES)]
            for d in range(DIRS):
                index = jnp.broadcast_to(inverse[t, pl.ds(d, 1), :], (rows, LANES))
                total = total + jnp.where(index >= 0, lane_gather(ret_in[q, d], index & (LANES - 1)), 0.0)
            for m in range(nmodes):
                total = total + levels[m] * modes_ref[pl.ds(m, 1), at]
            lam[g, :, at] = lam[g, :, at] + damping * total

    def iteration(it, carry):
        update(0, it - 1)
        halos(0, it)
        begin(0, it)
        rest(0, it)
        solve(it)
        return carry

    read_tables()
    halos(0, 0)
    build_operator(idx_ref, vals_ref, op_hi, op_lo, turned, low_rows)
    weights = 1.0 / (1.0 + code_ref[...].astype(f32))
    load_inverse.wait()
    chunk = 32

    def split_rows(number, carry):
        at = pl.ds(pl.multiple_of(number * chunk, chunk), chunk)
        high, low = split(li[at, :] * weights)
        li_hi[at, :] = high
        li_lo[at, :] = low
        return carry

    lax.fori_loop(0, block // chunk, split_rows, 0)
    begin(0, 0)
    rest(0, 0)
    solve(0)
    lax.fori_loop(1, ITERS, iteration, 0)
    update(0, ITERS - 1)
    for g in range(GROUPS):
        out_ref[g * rows : (g + 1) * rows, :] = lam[g]

    def drain(q, carry):
        for d in range(DIRS):

            @pl.when(inside(-direction_steps[d]))
            def _():
                halo_copy(q, d).wait_send()
                for step in range(cols):
                    mar_copy(q, d, step, c).wait_send()

        for step in range(1, cols):
            for part in range(len(cuts)):
                own_copy(q, part, step, c).wait_send()
        for by in range(1, subs):
            coarse_copy(q, by, s).wait_send()
        each_return(lambda d, step: ret_copy(q, d, step).wait_send())
        for b in range(cols):
            if own_parts[b]:

                @pl.when(c == b)
                def _():
                    for step in range(1, cols):
                        sol_copy(q, b, step).wait_send()

        return carry

    lax.fori_loop(0, ITERS * GROUPS, drain, 0)


def local(
    subs, cols,
    adjoint_source,
    start_field,
    row_diagonal,
    row_values,
    row_columns,
    weight_code,
    slot_count,
    slot_rows,
    local_inverse,
    coarse_modes,
    coarse_inverse,
):
    ncol, owned = start_field.shape
    block, ext = local_inverse.shape
    rows = ncol // GROUPS
    rounds = ITERS * GROUPS
    vmem = pl.BlockSpec(memory_space=pltpu.VMEM)
    dma = pltpu.SemaphoreType.DMA
    return pl.pallas_call(
        functools.partial(kernel, subs, cols),
        out_shape=jax.ShapeDtypeStruct((ncol, owned), f32),
        in_specs=[vmem] * 6 + [pl.BlockSpec(memory_space=pltpu.SMEM)] + [vmem] * 3 + [pl.BlockSpec(memory_space=pl.ANY)],
        out_specs=vmem,
        scratch_shapes=[
            pltpu.VMEM((GROUPS, rows, owned), f32),
            pltpu.VMEM((rows, owned), f32),
            pltpu.VMEM((ext, owned), bf16),
            pltpu.VMEM((ext, owned), bf16),
            pltpu.VMEM((3, owned, LANES), f32),
            pltpu.VMEM((SUBLANES // (LANES // (1 << (row_values.shape[0] - 1).bit_length())), owned // SUBLANES, LANES), f32),
            pltpu.VMEM((block, ext), f32),
            pltpu.VMEM((block, ext), bf16),
            pltpu.VMEM((block, ext), bf16),
            pltpu.VMEM((SUBLANES, LANES), jnp.int32),
            pltpu.VMEM((DIRS, SUBLANES, LANES), jnp.int32),
            pltpu.VMEM((SUBLANES, LANES), jnp.int32),
            pltpu.VMEM((owned // LANES, SUBLANES, LANES), jnp.int32),
            pltpu.VMEM((LANES, coarse_inverse.shape[1]), f32),
            pltpu.VMEM((coarse_inverse.shape[1], LANES), f32),
            pltpu.VMEM((rounds, DIRS, rows, LANES), f32),
            pltpu.VMEM((rounds, DIRS, rows, LANES), f32),
            pltpu.VMEM((rounds, cols, rows, owned), f32),
            pltpu.VMEM((rounds, DIRS, rows, LANES), f32),
            pltpu.VMEM((rounds, DIRS, cols, rows, LANES), f32),
            pltpu.VMEM((rounds, subs, rows, LANES), f32),
            pltpu.VMEM((rounds, cols, rows, block), f32),
            pltpu.VMEM((rounds, cols, rows, block), f32),
            pltpu.VMEM((rounds, DIRS, rows, LANES), f32),
            dma,
            dma((DIRS,)),
            dma((DIRS,)),
            dma((rounds, DIRS)),
            dma((rounds, DIRS)),
            dma((rounds, 2, cols)),
            dma((rounds, 2, cols)),
            dma((rounds, DIRS, cols)),
            dma((rounds, DIRS, cols)),
            dma((rounds, subs)),
            dma((rounds, subs)),
            dma((rounds, cols)),
            dma((rounds, cols)),
            dma((rounds, DIRS, cols)),
            dma((rounds, DIRS)),
        ],
        compiler_params=pltpu.CompilerParams(collective_id=0, has_side_effects=True),
    )(
        adjoint_source,
        start_field,
        row_diagonal.reshape(1, owned),
        row_values,
        row_columns,
        weight_code.reshape(1, ext),
        slot_count,
        slot_rows,
        coarse_modes,
        coarse_inverse,
        local_inverse,
    )


def solution(mesh):
    return jax.shard_map(
        functools.partial(local, mesh.shape["sub"], mesh.shape["col"]),
        mesh=mesh,
        in_specs=(
            P("col", "sub"),
            P("col", "sub"),
            P("sub"),
            P(None, "sub"),
            P(None, "sub"),
            P("sub"),
            P("sub", None),
            P("sub", None, None),
            P(("sub", "col"), None),
            P(None, "sub"),
            P("sub", None),
        ),
        out_specs=P("col", "sub"),
        check_vma=False,
    )
```

```python
import functools

import jax
import jax.numpy as jnp
from jax import lax
from jax.experimental import pallas as pl
from jax.experimental.pallas import tpu as pltpu
from jax.sharding import PartitionSpec as P

ITERS = 3
LANES = 128
SUBLANES = 8

direction_steps = (-2, -1, 1, 2)
damping = 0.7
highest = lax.Precision.HIGHEST
contract_last = (((1,), (1,)), ((), ()))
contract_first = (((1,), (0,)), ((), ()))
f32 = jnp.float32
bf16 = jnp.bfloat16
DIRS = len(direction_steps)
GROUPS = 1


def lane_gather(tile, low):
    return jnp.take_along_axis(tile, low, axis=1, mode="promise_in_bounds")


def split(x):
    high = x.astype(bf16)
    return high, (x - high.astype(f32)).astype(bf16)


def build_operator(idx_ref, vals_ref, op_hi, op_lo, turned, low_rows, halfway, later):
    terms, owned = idx_ref.shape
    heads = op_hi.shape[0] // LANES
    tiles = owned // LANES
    width = 1 << (terms - 1).bit_length()
    per = LANES // width
    halves = SUBLANES // per
    blocks = LANES // SUBLANES
    full = (LANES, LANES)
    square_row = lax.broadcasted_iota(jnp.int32, full, 0)
    square_lane = lax.broadcasted_iota(jnp.int32, full, 1)
    eye = jnp.where(square_row == square_lane, 1.0, 0.0).astype(bf16)
    keep = [square_row % SUBLANES == square_lane // width + per * h for h in range(halves)]
    few = (blocks, LANES)
    pick = lax.broadcasted_iota(jnp.int32, few, 1) // SUBLANES == lax.broadcasted_iota(jnp.int32, few, 0)
    pick = jnp.where(pick, 1.0, 0.0).astype(bf16)

    def turn(t, carry):
        at = pl.ds(pl.multiple_of(t * LANES, LANES), LANES)
        index, value = idx_ref[:, at], vals_ref[:, at]

        def tiled(x, fill):
            x = jnp.concatenate([x, jnp.full((width - terms, LANES), fill, f32)], axis=0)
            return jnp.concatenate([x] * per, axis=0).astype(bf16)

        def turn_one(x):
            return lax.dot_general(eye, x, contract_last, preferred_element_type=f32)

        top = value.astype(bf16).astype(f32)
        turned[0, at, :] = turn_one(tiled((index >> 7).astype(f32), -1.0))
        turned[1, at, :] = turn_one(tiled(top, 0.0))
        turned[2, at, :] = turn_one(tiled(value - top, 0.0))
        low = turn_one(tiled((index & (LANES - 1)).astype(f32), -1.0))
        for h in range(halves):
            low_rows[h, pl.ds(pl.multiple_of(t * blocks, blocks), blocks), :] = lax.dot_general(
                pick, jnp.where(keep[h], low, 0.0).astype(bf16), contract_first, preferred_element_type=f32
            )
        return carry

    lax.fori_loop(0, tiles, turn, 0, unroll=tiles)

    halfway()
    lane_number = square_row.astype(f32).astype(bf16)
    tall = (heads * SUBLANES, LANES)
    head_number = (lax.broadcasted_iota(jnp.int32, tall, 0) // SUBLANES).astype(f32).astype(bf16)
    small = (SUBLANES, LANES)
    mine = [
        lax.broadcasted_iota(jnp.int32, small, 0) == lax.broadcasted_iota(jnp.int32, small, 1) // width + per * h
        for h in range(halves)
    ]
    one, zero = jnp.ones(full, bf16), jnp.zeros(full, bf16)
    none = jnp.zeros(tall, bf16)

    def repeat(x):
        pair = jnp.concatenate([x, x], axis=0).astype(bf16)
        return jnp.concatenate([pair] * (heads // 2), axis=0)

    def one_block(row):
        at = pl.ds(pl.multiple_of(row * SUBLANES, SUBLANES), SUBLANES)
        head = turned[0, at, :]
        value_hi, value_lo = repeat(turned[1, at, :]), repeat(turned[2, at, :])
        left_hi, left_lo, right = [], [], []
        for h in range(halves):
            hit = repeat(jnp.where(mine[h], head, -1.0)) == head_number
            left_hi.append(jnp.where(hit, value_hi, none))
            left_lo.append(jnp.where(hit, value_lo, none))
            low = jnp.broadcast_to(low_rows[h, pl.ds(row, 1), :], (2 * SUBLANES, LANES)).astype(bf16)
            low = jnp.concatenate([low] * (LANES // (2 * SUBLANES)), axis=0)
            right.append(jnp.where(low == lane_number, one, zero))
        left = jnp.concatenate([jnp.concatenate(left_hi, axis=1), jnp.concatenate(left_lo, axis=1)], axis=0)
        out = lax.dot_general(left, jnp.concatenate(right, axis=1), contract_last, preferred_element_type=f32)
        return out[: heads * SUBLANES] + out[heads * SUBLANES :]

    def one_tile(t, carry):
        at = pl.ds(pl.multiple_of(t * LANES, LANES), LANES)
        outs = [one_block(t * blocks + b) for b in range(blocks)]
        for h in range(heads):
            x = jnp.concatenate([out[h * SUBLANES : (h + 1) * SUBLANES] for out in outs], axis=0).T
            high, low = split(x)
            op_hi[h * LANES : (h + 1) * LANES, at] = high
            op_lo[h * LANES : (h + 1) * LANES, at] = low
        return carry

    early = tiles // 4 * 2
    lax.fori_loop(0, early, one_tile, 0, unroll=2)
    later()
    lax.fori_loop(early, tiles, one_tile, 0, unroll=2)


def kernel(
    subs, cols,
    source_ref, start_ref, diag_ref, vals_ref, idx_ref, code_ref, count_ref, rows_ref, modes_ref, cinv_ref, li_hbm,
    out_ref,
    lam, base, op_hi, op_lo, turned, low_rows, li, li_hi, li_lo, weights_ref, table, tables, fidx, inverse, cinv_pad, cinv_turned,
    halo_out, halo_in, own_x, mar_out, mar_x, coarse_x, solved, sol_in, ret_in,
    li_sem, tab_s, tab_r, halo_s, halo_r, own_s, own_r, mar_s, mar_r, co_s, co_r, sol_s, sol_r, ret_s, ret_r,
):
    s = lax.axis_index("sub")
    c = lax.axis_index("col")
    owned = start_ref.shape[1]
    rows = lam.shape[1]
    tiles = owned // LANES
    early = tiles // 2
    block = li_hbm.shape[0]
    nmodes = modes_ref.shape[0]
    cuts = ((0, early * LANES), (early * LANES, owned - early * LANES))

    def sub_at(by):
        return lax.rem(s + (by + subs), subs)

    def col_at(by):
        return lax.rem(c + (by + cols), cols)

    def inside(by):
        return jnp.logical_and(s + by >= 0, s + by < subs)

    def remote(src, dst, send, recv, where):
        return pltpu.make_async_remote_copy(
            src_ref=src, dst_ref=dst, send_sem=send, recv_sem=recv,
            device_id=where, device_id_type=pl.DeviceIdType.MESH,
        )

    load_inverse = pltpu.make_async_copy(li_hbm, li, li_sem)
    load_inverse.start()

    partners = []
    for step in range(1, cols):
        partners.append((0, step))
    for by in range(1, subs):
        near = by in (1, 2, subs - 1, subs - 2)
        for step in range(cols if near else 1):
            partners.append((by, step))
    barrier = pltpu.get_barrier_semaphore()
    tables[...] = jnp.full(tables.shape, -1, jnp.int32)
    for clean in (halo_in, mar_x, ret_in, coarse_x):
        clean[...] = jnp.zeros_like(clean)
    for by, step in partners:
        pl.semaphore_signal(
            barrier, inc=1, device_id=(sub_at(by), col_at(step)), device_id_type=pl.DeviceIdType.MESH
        )
    lane = lax.broadcasted_iota(jnp.int32, (1, LANES), 1)
    for d in range(DIRS):
        table[pl.ds(d, 1), :] = jnp.where(lane < count_ref[0, d], rows_ref[0, pl.ds(d, 1), :], -1)
    for g in range(GROUPS):
        lam[g] = start_ref[g * rows : (g + 1) * rows, :]
    members = subs * nmodes
    cinv_pad[...] = jnp.zeros_like(cinv_pad)
    cinv_pad[pl.ds(0, nmodes), :] = cinv_ref[...]
    square = (members, members)
    same = lax.broadcasted_iota(jnp.int32, square, 0) == lax.broadcasted_iota(jnp.int32, square, 1)
    cinv_turned[...] = lax.dot_general(
        jnp.where(same, 1.0, 0.0), cinv_pad[...], contract_last, precision=highest, preferred_element_type=f32
    )

    def tab_copy(d):
        return remote(table, tables.at[d], tab_s.at[d], tab_r.at[d], (sub_at(direction_steps[d]), c))

    def send_tables():
        pl.semaphore_wait(barrier, len(partners))
        for d in range(DIRS):

            @pl.when(inside(direction_steps[d]))
            def _():
                tab_copy(d).start()

    def read_tables():
        for d in range(DIRS):

            @pl.when(inside(direction_steps[d]))
            def _():
                tab_copy(d).wait_send()

            @pl.when(inside(-direction_steps[d]))
            def _():
                tab_copy(d).wait_recv()

        for d in range(DIRS):
            fidx[pl.ds(d, 1), :] = tables[d, pl.ds(d, 1), :]

        slot_number = lax.broadcasted_iota(jnp.int32, (LANES, LANES), 0).astype(f32) + 1.0
        lane_full = lax.broadcasted_iota(jnp.int32, (LANES, LANES), 1).astype(f32)
        for d in range(DIRS):
            wanted = jnp.broadcast_to(fidx[pl.ds(d, 1), :].astype(f32), (LANES, LANES)).T

            def invert(number, carry):
                hit = wanted == lane_full + lax.convert_element_type(number * LANES, f32)
                found = jnp.sum(jnp.where(hit, slot_number, 0.0), axis=0, keepdims=True)
                inverse[number, pl.ds(d, 1), :] = found.astype(jnp.int32) - 1
                return carry

            lax.fori_loop(0, tiles, invert, 0)

    def pack(read_tile, put):
        for d in range(DIRS):
            index = jnp.broadcast_to(fidx[pl.ds(d, 1), :], (rows, LANES))
            low, high = index & (LANES - 1), index >> 7
            total = jnp.zeros((rows, LANES), f32)
            for t in range(tiles):
                total = jnp.where(high == t, lane_gather(read_tile(t), low), total)
            put(d, total)

    def operate(x, low, high, at):
        count = x.shape[0]
        top, bottom = split(x)
        stretch = pl.ds(low, high - low)
        both = jnp.dot(jnp.concatenate([top, bottom], axis=0), op_hi[stretch, at], preferred_element_type=f32)
        cross = jnp.dot(top, op_lo[stretch, at], preferred_element_type=f32)
        return both[:count] + (both[count:] + cross)

    own_parts = [max(0, min((b + 1) * block, owned) - b * block) for b in range(cols)]
    slot_homes = [divmod(owned + d * LANES, block) for d in range(DIRS)]

    def halo_copy(q, d):
        return remote(
            halo_out.at[q, d], halo_in.at[q, d], halo_s.at[q, d], halo_r.at[q, d], (sub_at(-direction_steps[d]), c)
        )

    sibling = c + 1 - 2 * lax.rem(c, 2)

    def own_copy(q, part, step, slot):
        piece = own_x.at[q, slot, :, pl.ds(*cuts[part])]
        where = sibling if step % 2 else col_at(step)
        return remote(piece, piece, own_s.at[q, part, step], own_r.at[q, part, step], (s, where))

    def passed(step):
        return c if step == 1 else col_at(1 - step)

    def came(step):
        return lax.rem(sibling + (1 - step + cols), cols) if step % 2 else col_at(-step)

    def forward(q):
        for part in range(len(cuts)):
            for step in range(2, cols, 2):
                own_copy(q, part, step, came(step)).wait_recv()
                own_copy(q, part, step + 1, passed(step + 1)).start()

    def mar_copy(q, d, step, slot):
        return remote(
            mar_out.at[q, d], mar_x.at[q, d, slot], mar_s.at[q, d, step], mar_r.at[q, d, step],
            (sub_at(-direction_steps[d]), col_at(step)),
        )

    def coarse_copy(q, by, slot):
        return remote(coarse_x.at[q, slot], coarse_x.at[q, slot], co_s.at[q, by], co_r.at[q, by], (sub_at(by), c))

    def sol_copy(q, b, step):
        width = own_parts[b]
        return remote(
            solved.at[q, col_at(step), :, pl.ds(0, width)], sol_in.at[q, b, :, pl.ds(0, width)],
            sol_s.at[q, step], sol_r.at[q, b], (s, col_at(step)),
        )

    def ret_copy(q, d, step):
        return remote(
            solved.at[q, col_at(step), :, pl.ds(slot_homes[d][1], LANES)], ret_in.at[q, d],
            ret_s.at[q, d, step], ret_r.at[q, d], (sub_at(direction_steps[d]), col_at(step)),
        )

    def each_return(act):
        for d in range(DIRS):

            @pl.when(jnp.logical_and(c == slot_homes[d][0], inside(direction_steps[d])))
            def _():
                for step in range(cols):
                    act(d, step)

    def halos(g, q):
        def put_halo(d, total):
            halo_out[q, d] = total

            @pl.when(inside(-direction_steps[d]))
            def _():
                halo_copy(q, d).start()

        pack(lambda t: lam[g, :, t * LANES : (t + 1) * LANES], put_halo)

    def begin(g, q):
        for low, count in cuts:
            at = pl.ds(low, count)
            held = lam[g, :, at]
            base[:, at] = source_ref[g * rows : (g + 1) * rows, at] - diag_ref[:, at] * held - operate(lam[g], 0, owned, at)

    def rest(g, q):
        for d in range(DIRS):

            @pl.when(inside(direction_steps[d]))
            def _():
                halo_copy(q, d).wait_recv()

        slots = jnp.concatenate([halo_in[q, d] for d in range(DIRS)], axis=1)
        for part, (low, count) in enumerate(cuts):
            at = pl.ds(low, count)
            own_x[q, c, :, at] = base[:, at] - operate(slots, owned, owned + DIRS * LANES, at)
            for step in [*range(2, cols, 2), 1]:
                own_copy(q, part, step, c).start()

        def put_margin(d, total):
            mar_out[q, d] = total

            @pl.when(inside(-direction_steps[d]))
            def _():
                for step in range(cols):
                    mar_copy(q, d, step, c).start()

        pack(lambda t: own_x[q, c, :, t * LANES : (t + 1) * LANES], put_margin)
        message = jnp.zeros((rows, LANES), f32)
        for m in range(nmodes):
            part = jnp.zeros((rows, LANES), f32)
            for t in range(tiles):
                at = pl.ds(t * LANES, LANES)
                part = part + own_x[q, c, :, at] * modes_ref[pl.ds(m, 1), at]
            message = jnp.where(lane == m, jnp.sum(part, axis=1, keepdims=True), message)
        coarse_x[q, s] = message
        for by in range(1, subs):
            coarse_copy(q, by, s).start()

    def product(x, at):
        high, low = split(x)
        count = x.shape[0]
        both = jnp.dot(jnp.concatenate([high, low], axis=0), li_hi[at, :], preferred_element_type=f32)
        cross = jnp.dot(high, li_lo[at, :], preferred_element_type=f32)
        return both[:count] + (both[count:] + cross)

    def solve(q):
        total = jnp.zeros((cols * rows, block), f32)
        for part, (low, count) in enumerate(cuts):
            for step in range(1, cols, 2):
                own_copy(q, part, step, came(step)).wait_recv()
            at = pl.ds(low, count)
            total = total + product(own_x[q, :, :, at].reshape(cols * rows, count), at)
        for d in range(DIRS):

            @pl.when(inside(direction_steps[d]))
            def _():
                for step in range(cols):
                    mar_copy(q, d, step, col_at(-step)).wait_recv()

        margins = jnp.concatenate([mar_x[q, d].reshape(cols * rows, LANES) for d in range(DIRS)], axis=1)
        total = total + product(margins, pl.ds(owned, DIRS * LANES))
        solved[q] = total.reshape(cols, rows, block)
        each_return(lambda d, step: ret_copy(q, d, step).start())
        for b in range(cols):
            if own_parts[b]:

                @pl.when(c == b)
                def _():
                    for step in range(1, cols):
                        sol_copy(q, b, step).start()
                    sol_in[q, b, :, pl.ds(0, own_parts[b])] = solved[q, c, :, pl.ds(0, own_parts[b])]

    def update(g, q):
        for by in range(1, subs):
            coarse_copy(q, by, sub_at(-by)).wait_recv()
        coarse = jnp.zeros((rows, LANES), f32)
        for other in range(subs):
            message = coarse_x[q, other]
            for m in range(nmodes):
                coarse = coarse + message[:, m : m + 1] * cinv_turned[pl.ds(other * nmodes + m, 1), :]
        levels = [jnp.broadcast_to(coarse[:, m : m + 1], (rows, LANES)) for m in range(nmodes)]
        for b in range(cols):
            if own_parts[b]:

                @pl.when(c != b)
                def _():
                    sol_copy(q, b, 0).wait_recv()

        for d in range(DIRS):

            @pl.when(inside(-direction_steps[d]))
            def _():
                ret_copy(q, d, 0).wait_recv()

        for t in range(tiles):
            at = pl.ds(t * LANES, LANES)
            b, offset = divmod(t * LANES, block)
            total = sol_in[q, b, :, pl.ds(offset, LANES)]
            for d in range(DIRS):
                index = jnp.broadcast_to(inverse[t, pl.ds(d, 1), :], (rows, LANES))
                total = total + jnp.where(index >= 0, lane_gather(ret_in[q, d], index & (LANES - 1)), 0.0)
            for m in range(nmodes):
                total = total + levels[m] * modes_ref[pl.ds(m, 1), at]
            lam[g, :, at] = lam[g, :, at] + damping * total

    def iteration(it, carry):
        update(0, it - 1)
        halos(0, it)
        begin(0, it)
        rest(0, it)
        forward(it)
        solve(it)
        return carry

    def start_halos():
        read_tables()
        for g in range(GROUPS):
            halos(g, g)

    build_operator(idx_ref, vals_ref, op_hi, op_lo, turned, low_rows, send_tables, start_halos)
    weights_ref[...] = 1.0 / (1.0 + code_ref[...].astype(f32))
    load_inverse.wait()

    def split_tile(number, carry):
        at = pl.ds(pl.multiple_of(number * LANES, LANES), LANES)
        scale = weights_ref[:, at]
        for low in range(0, block, LANES):
            high, rest_of = split((li[low : low + LANES, at] * scale).T)
            li_hi[at, low : low + LANES] = high
            li_lo[at, low : low + LANES] = rest_of
        return carry

    lax.fori_loop(0, li_hbm.shape[1] // LANES, split_tile, 0, unroll=2)
    begin(0, 0)
    rest(0, 0)
    forward(0)
    solve(0)
    lax.fori_loop(1, ITERS, iteration, 0)
    update(0, ITERS - 1)
    for g in range(GROUPS):
        out_ref[g * rows : (g + 1) * rows, :] = lam[g]

    def drain(q, carry):
        for d in range(DIRS):

            @pl.when(inside(-direction_steps[d]))
            def _():
                halo_copy(q, d).wait_send()
                for step in range(cols):
                    mar_copy(q, d, step, c).wait_send()

        for step in range(1, cols):
            for part in range(len(cuts)):
                own_copy(q, part, step, passed(step) if step % 2 else c).wait_send()
        for by in range(1, subs):
            coarse_copy(q, by, s).wait_send()
        each_return(lambda d, step: ret_copy(q, d, step).wait_send())
        for b in range(cols):
            if own_parts[b]:

                @pl.when(c == b)
                def _():
                    for step in range(1, cols):
                        sol_copy(q, b, step).wait_send()

        return carry

    lax.fori_loop(0, ITERS * GROUPS, drain, 0)


def local(
    subs, cols,
    adjoint_source,
    start_field,
    row_diagonal,
    row_values,
    row_columns,
    weight_code,
    slot_count,
    slot_rows,
    local_inverse,
    coarse_modes,
    coarse_inverse,
):
    ncol, owned = start_field.shape
    block, ext = local_inverse.shape
    rows = ncol // GROUPS
    rounds = ITERS * GROUPS
    vmem = pl.BlockSpec(memory_space=pltpu.VMEM)
    dma = pltpu.SemaphoreType.DMA
    return pl.pallas_call(
        functools.partial(kernel, subs, cols),
        out_shape=jax.ShapeDtypeStruct((ncol, owned), f32),
        in_specs=[vmem] * 6 + [pl.BlockSpec(memory_space=pltpu.SMEM)] + [vmem] * 3 + [pl.BlockSpec(memory_space=pl.ANY)],
        out_specs=vmem,
        scratch_shapes=[
            pltpu.VMEM((GROUPS, rows, owned), f32),
            pltpu.VMEM((rows, owned), f32),
            pltpu.VMEM((ext, owned), bf16),
            pltpu.VMEM((ext, owned), bf16),
            pltpu.VMEM((3, owned, LANES), f32),
            pltpu.VMEM((SUBLANES // (LANES // (1 << (row_values.shape[0] - 1).bit_length())), owned // SUBLANES, LANES), f32),
            pltpu.VMEM((block, ext), f32),
            pltpu.VMEM((ext, block), bf16),
            pltpu.VMEM((ext, block), bf16),
            pltpu.VMEM((1, ext), f32),
            pltpu.VMEM((SUBLANES, LANES), jnp.int32),
            pltpu.VMEM((DIRS, SUBLANES, LANES), jnp.int32),
            pltpu.VMEM((SUBLANES, LANES), jnp.int32),
            pltpu.VMEM((owned // LANES, SUBLANES, LANES), jnp.int32),
            pltpu.VMEM((LANES, coarse_inverse.shape[1]), f32),
            pltpu.VMEM((coarse_inverse.shape[1], LANES), f32),
            pltpu.VMEM((rounds, DIRS, rows, LANES), f32),
            pltpu.VMEM((rounds, DIRS, rows, LANES), f32),
            pltpu.VMEM((rounds, cols, rows, owned), f32),
            pltpu.VMEM((rounds, DIRS, rows, LANES), f32),
            pltpu.VMEM((rounds, DIRS, cols, rows, LANES), f32),
            pltpu.VMEM((rounds, subs, rows, LANES), f32),
            pltpu.VMEM((rounds, cols, rows, block), f32),
            pltpu.VMEM((rounds, cols, rows, block), f32),
            pltpu.VMEM((rounds, DIRS, rows, LANES), f32),
            dma,
            dma((DIRS,)),
            dma((DIRS,)),
            dma((rounds, DIRS)),
            dma((rounds, DIRS)),
            dma((rounds, 2, cols)),
            dma((rounds, 2, cols)),
            dma((rounds, DIRS, cols)),
            dma((rounds, DIRS, cols)),
            dma((rounds, subs)),
            dma((rounds, subs)),
            dma((rounds, cols)),
            dma((rounds, cols)),
            dma((rounds, DIRS, cols)),
            dma((rounds, DIRS)),
        ],
        compiler_params=pltpu.CompilerParams(collective_id=0, has_side_effects=True),
    )(
        adjoint_source,
        start_field,
        row_diagonal.reshape(1, owned),
        row_values,
        row_columns,
        weight_code.reshape(1, ext),
        slot_count,
        slot_rows,
        coarse_modes,
        coarse_inverse,
        local_inverse,
    )


def solution(mesh):
    return jax.shard_map(
        functools.partial(local, mesh.shape["sub"], mesh.shape["col"]),
        mesh=mesh,
        in_specs=(
            P("col", "sub"),
            P("col", "sub"),
            P("sub"),
            P(None, "sub"),
            P(None, "sub"),
            P("sub"),
            P("sub", None),
            P("sub", None, None),
            P(("sub", "col"), None),
            P(None, "sub"),
            P("sub", None),
        ),
        out_specs=P("col", "sub"),
        check_vma=False,
    )
```

```python
import functools

import jax
import jax.numpy as jnp
from jax import lax
from jax.experimental import pallas as pl
from jax.experimental.pallas import tpu as pltpu
from jax.sharding import PartitionSpec as P

ITERS = 3
LANES = 128
SUBLANES = 8

direction_steps = (-2, -1, 1, 2)
damping = 0.7
highest = lax.Precision.HIGHEST
contract_last = (((1,), (1,)), ((), ()))
contract_first = (((1,), (0,)), ((), ()))
f32 = jnp.float32
bf16 = jnp.bfloat16
DIRS = len(direction_steps)
GROUPS = 1


def lane_gather(tile, low):
    return jnp.take_along_axis(tile, low, axis=1, mode="promise_in_bounds")


def split(x):
    high = x.astype(bf16)
    return high, (x - high.astype(f32)).astype(bf16)


def build_operator(idx_ref, vals_ref, op_hi, op_lo, turned, low_rows, halfway, later, beside):
    terms, owned = idx_ref.shape
    heads = op_hi.shape[0] // LANES
    tiles = owned // LANES
    width = 1 << (terms - 1).bit_length()
    per = LANES // width
    halves = SUBLANES // per
    blocks = LANES // SUBLANES
    full = (LANES, LANES)
    square_row = lax.broadcasted_iota(jnp.int32, full, 0)
    square_lane = lax.broadcasted_iota(jnp.int32, full, 1)
    eye = jnp.where(square_row == square_lane, 1.0, 0.0).astype(bf16)
    keep = [square_row % SUBLANES == square_lane // width + per * h for h in range(halves)]
    few = (blocks, LANES)
    pick = lax.broadcasted_iota(jnp.int32, few, 1) // SUBLANES == lax.broadcasted_iota(jnp.int32, few, 0)
    pick = jnp.where(pick, 1.0, 0.0).astype(bf16)

    def turn(t, carry):
        at = pl.ds(pl.multiple_of(t * LANES, LANES), LANES)
        index, value = idx_ref[:, at], vals_ref[:, at]

        def tiled(x, fill):
            x = jnp.concatenate([x, jnp.full((width - terms, LANES), fill, f32)], axis=0)
            return jnp.concatenate([x] * per, axis=0).astype(bf16)

        def turn_one(x):
            return lax.dot_general(eye, x, contract_last, preferred_element_type=f32)

        top = value.astype(bf16).astype(f32)
        turned[0, at, :] = turn_one(tiled((index >> 7).astype(f32), -1.0))
        turned[1, at, :] = turn_one(tiled(top, 0.0))
        turned[2, at, :] = turn_one(tiled(value - top, 0.0))
        low = turn_one(tiled((index & (LANES - 1)).astype(f32), -1.0))
        for h in range(halves):
            low_rows[h, pl.ds(pl.multiple_of(t * blocks, blocks), blocks), :] = lax.dot_general(
                pick, jnp.where(keep[h], low, 0.0).astype(bf16), contract_first, preferred_element_type=f32
            )
        return carry

    lax.fori_loop(0, tiles, turn, 0, unroll=tiles)

    halfway()
    lane_number = square_row.astype(f32).astype(bf16)
    tall = (heads * SUBLANES, LANES)
    head_number = (lax.broadcasted_iota(jnp.int32, tall, 0) // SUBLANES).astype(f32).astype(bf16)
    small = (SUBLANES, LANES)
    mine = [
        lax.broadcasted_iota(jnp.int32, small, 0) == lax.broadcasted_iota(jnp.int32, small, 1) // width + per * h
        for h in range(halves)
    ]
    one, zero = jnp.ones(full, bf16), jnp.zeros(full, bf16)
    none = jnp.zeros(tall, bf16)

    def repeat(x):
        pair = jnp.concatenate([x, x], axis=0).astype(bf16)
        return jnp.concatenate([pair] * (heads // 2), axis=0)

    def one_block(row):
        at = pl.ds(pl.multiple_of(row * SUBLANES, SUBLANES), SUBLANES)
        head = turned[0, at, :]
        value_hi, value_lo = repeat(turned[1, at, :]), repeat(turned[2, at, :])
        left_hi, left_lo, right = [], [], []
        for h in range(halves):
            hit = repeat(jnp.where(mine[h], head, -1.0)) == head_number
            left_hi.append(jnp.where(hit, value_hi, none))
            left_lo.append(jnp.where(hit, value_lo, none))
            low = jnp.broadcast_to(low_rows[h, pl.ds(row, 1), :], (2 * SUBLANES, LANES)).astype(bf16)
            low = jnp.concatenate([low] * (LANES // (2 * SUBLANES)), axis=0)
            right.append(jnp.where(low == lane_number, one, zero))
        left = jnp.concatenate([jnp.concatenate(left_hi, axis=1), jnp.concatenate(left_lo, axis=1)], axis=0)
        out = lax.dot_general(left, jnp.concatenate(right, axis=1), contract_last, preferred_element_type=f32)
        return out[: heads * SUBLANES] + out[heads * SUBLANES :]

    def one_tile(t, carry):
        at = pl.ds(pl.multiple_of(t * LANES, LANES), LANES)
        outs = [one_block(t * blocks + b) for b in range(blocks)]
        for h in range(heads):
            x = jnp.concatenate([out[h * SUBLANES : (h + 1) * SUBLANES] for out in outs], axis=0).T
            high, low = split(x)
            op_hi[h * LANES : (h + 1) * LANES, at] = high
            op_lo[h * LANES : (h + 1) * LANES, at] = low
        return carry

    early = tiles // 4 * 2
    lax.fori_loop(0, early, one_tile, 0, unroll=2)
    later()

    def one_tile_beside(t, carry):
        beside(t - early, tiles - early)
        return one_tile(t, carry)

    lax.fori_loop(early, tiles, one_tile_beside, 0, unroll=2)


def kernel(
    subs, cols,
    source_ref, start_ref, diag_ref, vals_ref, idx_ref, code_ref, count_ref, rows_ref, modes_ref, cinv_ref, li_hbm,
    out_ref,
    lam, diag, base, op_hi, op_lo, turned, low_rows, li, li_hi, li_lo, weights_ref, table, tables, fidx, inverse, cinv_pad, cinv_turned,
    halo_out, halo_in, own_x, mar_out, mar_x, coarse_x, solved, sol_in, ret_in,
    li_sem, tab_s, tab_r, halo_s, halo_r, own_s, own_r, mar_s, mar_r, co_s, co_r, sol_s, sol_r, ret_s, ret_r,
):
    s = lax.axis_index("sub")
    c = lax.axis_index("col")
    owned = start_ref.shape[1]
    rows = lam.shape[1]
    tiles = owned // LANES
    block = li_hbm.shape[0]
    nmodes = modes_ref.shape[0]
    pieces = 3
    edges = [tiles * n // pieces * LANES for n in range(pieces + 1)]
    cuts = tuple((low, high - low) for low, high in zip(edges, edges[1:]))

    def sub_at(by):
        return lax.rem(s + (by + subs), subs)

    def col_at(by):
        return lax.rem(c + (by + cols), cols)

    def inside(by):
        return jnp.logical_and(s + by >= 0, s + by < subs)

    def remote(src, dst, send, recv, where):
        return pltpu.make_async_remote_copy(
            src_ref=src, dst_ref=dst, send_sem=send, recv_sem=recv,
            device_id=where, device_id_type=pl.DeviceIdType.MESH,
        )

    load_inverse = pltpu.make_async_copy(li_hbm, li, li_sem)
    load_inverse.start()

    partners = []
    for step in range(1, cols):
        partners.append((0, step))
    for by in range(1, subs):
        near = by in (1, 2, subs - 1, subs - 2)
        for step in range(cols if near else 1):
            partners.append((by, step))
    barrier = pltpu.get_barrier_semaphore()
    tables[...] = jnp.full(tables.shape, -1, jnp.int32)
    for clean in (halo_in, mar_x, ret_in, coarse_x):
        clean[...] = jnp.zeros_like(clean)
    for by, step in partners:
        pl.semaphore_signal(
            barrier, inc=1, device_id=(sub_at(by), col_at(step)), device_id_type=pl.DeviceIdType.MESH
        )
    lane = lax.broadcasted_iota(jnp.int32, (1, LANES), 1)
    for d in range(DIRS):
        table[pl.ds(d, 1), :] = jnp.where(lane < count_ref[0, d], rows_ref[0, pl.ds(d, 1), :], -1)
    for t in range(tiles):
        diag[:, t * LANES : (t + 1) * LANES] = diag_ref[pl.ds(t * LANES, LANES)].reshape(1, LANES)
    for g in range(GROUPS):
        lam[g] = start_ref[g * rows : (g + 1) * rows, :]
    members = subs * nmodes
    cinv_pad[...] = jnp.zeros_like(cinv_pad)
    cinv_pad[pl.ds(0, nmodes), :] = cinv_ref[...]
    square = (members, members)
    same = lax.broadcasted_iota(jnp.int32, square, 0) == lax.broadcasted_iota(jnp.int32, square, 1)
    cinv_turned[...] = lax.dot_general(
        jnp.where(same, 1.0, 0.0), cinv_pad[...], contract_last, precision=highest, preferred_element_type=f32
    )

    def tab_copy(d):
        return remote(table, tables.at[d], tab_s.at[d], tab_r.at[d], (sub_at(direction_steps[d]), c))

    def send_tables():
        pl.semaphore_wait(barrier, len(partners))
        for d in range(DIRS):

            @pl.when(inside(direction_steps[d]))
            def _():
                tab_copy(d).start()

    def read_tables():
        for d in range(DIRS):

            @pl.when(inside(direction_steps[d]))
            def _():
                tab_copy(d).wait_send()

            @pl.when(inside(-direction_steps[d]))
            def _():
                tab_copy(d).wait_recv()

        for d in range(DIRS):
            fidx[pl.ds(d, 1), :] = tables[d, pl.ds(d, 1), :]

        slot_number = lax.broadcasted_iota(jnp.int32, (LANES, LANES), 0).astype(f32) + 1.0
        lane_full = lax.broadcasted_iota(jnp.int32, (LANES, LANES), 1).astype(f32)
        for d in range(DIRS):
            wanted = jnp.broadcast_to(fidx[pl.ds(d, 1), :].astype(f32), (LANES, LANES)).T

            def invert(number, carry):
                hit = wanted == lane_full + lax.convert_element_type(number * LANES, f32)
                found = jnp.sum(jnp.where(hit, slot_number, 0.0), axis=0, keepdims=True)
                inverse[number, pl.ds(d, 1), :] = found.astype(jnp.int32) - 1
                return carry

            lax.fori_loop(0, tiles, invert, 0, unroll=4)

    def pack(read_tile, put):
        for d in range(DIRS):
            index = jnp.broadcast_to(fidx[pl.ds(d, 1), :], (rows, LANES))
            low, high = index & (LANES - 1), index >> 7
            total = jnp.zeros((rows, LANES), f32)
            for t in range(tiles):
                total = jnp.where(high == t, lane_gather(read_tile(t), low), total)
            put(d, total)

    def operate(x, low, high, at):
        count = x.shape[0]
        top, bottom = split(x)
        stretch = pl.ds(low, high - low)
        both = jnp.dot(jnp.concatenate([top, bottom], axis=0), op_hi[stretch, at], preferred_element_type=f32)
        cross = jnp.dot(top, op_lo[stretch, at], preferred_element_type=f32)
        return both[:count] + (both[count:] + cross)

    own_parts = [max(0, min((b + 1) * block, owned) - b * block) for b in range(cols)]
    slot_homes = [divmod(owned + d * LANES, block) for d in range(DIRS)]

    def halo_copy(q, d):
        return remote(
            halo_out.at[q, d], halo_in.at[q, d], halo_s.at[q, d], halo_r.at[q, d], (sub_at(-direction_steps[d]), c)
        )

    sibling = c + 1 - 2 * lax.rem(c, 2)

    def own_copy(q, part, step, slot):
        piece = own_x.at[q, slot, :, pl.ds(*cuts[part])]
        where = sibling if step % 2 else col_at(step)
        return remote(piece, piece, own_s.at[q, part, step], own_r.at[q, part, step], (s, where))

    def passed(step):
        return c if step == 1 else col_at(1 - step)

    def came(step):
        return lax.rem(sibling + (1 - step + cols), cols) if step % 2 else col_at(-step)

    def forward(q):
        for part in range(len(cuts)):
            for step in range(2, cols, 2):
                own_copy(q, part, step, came(step)).wait_recv()
                own_copy(q, part, step + 1, passed(step + 1)).start()

    def mar_copy(q, d, step, slot):
        return remote(
            mar_out.at[q, d], mar_x.at[q, d, slot], mar_s.at[q, d, step], mar_r.at[q, d, step],
            (sub_at(-direction_steps[d]), col_at(step)),
        )

    def coarse_copy(q, by, slot):
        return remote(coarse_x.at[q, slot], coarse_x.at[q, slot], co_s.at[q, by], co_r.at[q, by], (sub_at(by), c))

    def sol_copy(q, b, step):
        width = own_parts[b]
        return remote(
            solved.at[q, col_at(step), :, pl.ds(0, width)], sol_in.at[q, b, :, pl.ds(0, width)],
            sol_s.at[q, step], sol_r.at[q, b], (s, col_at(step)),
        )

    def ret_copy(q, d, step):
        return remote(
            solved.at[q, col_at(step), :, pl.ds(slot_homes[d][1], LANES)], ret_in.at[q, d],
            ret_s.at[q, d, step], ret_r.at[q, d], (sub_at(direction_steps[d]), col_at(step)),
        )

    def each_return(act):
        for d in range(DIRS):

            @pl.when(jnp.logical_and(c == slot_homes[d][0], inside(direction_steps[d])))
            def _():
                for step in range(cols):
                    act(d, step)

    def halos(g, q):
        def put_halo(d, total):
            halo_out[q, d] = total

            @pl.when(inside(-direction_steps[d]))
            def _():
                halo_copy(q, d).start()

        pack(lambda t: lam[g, :, t * LANES : (t + 1) * LANES], put_halo)

    def begin(g, q):
        for low, count in cuts:
            at = pl.ds(low, count)
            held = lam[g, :, at]
            base[:, at] = source_ref[g * rows : (g + 1) * rows, at] - diag[:, at] * held - operate(lam[g], 0, owned, at)

    def rest(g, q):
        for d in range(DIRS):

            @pl.when(inside(direction_steps[d]))
            def _():
                halo_copy(q, d).wait_recv()

        slots = jnp.concatenate([halo_in[q, d] for d in range(DIRS)], axis=1)
        for part, (low, count) in enumerate(cuts):
            at = pl.ds(low, count)
            own_x[q, c, :, at] = base[:, at] - operate(slots, owned, owned + DIRS * LANES, at)
            for step in [*range(2, cols, 2), 1]:
                own_copy(q, part, step, c).start()

        def put_margin(d, total):
            mar_out[q, d] = total

            @pl.when(inside(-direction_steps[d]))
            def _():
                for step in range(cols):
                    mar_copy(q, d, step, c).start()

        pack(lambda t: own_x[q, c, :, t * LANES : (t + 1) * LANES], put_margin)
        message = jnp.zeros((rows, LANES), f32)
        for m in range(nmodes):
            part = jnp.zeros((rows, LANES), f32)
            for t in range(tiles):
                at = pl.ds(t * LANES, LANES)
                part = part + own_x[q, c, :, at] * modes_ref[pl.ds(m, 1), at]
            message = jnp.where(lane == m, jnp.sum(part, axis=1, keepdims=True), message)
        coarse_x[q, s] = message
        for by in range(1, subs):
            coarse_copy(q, by, s).start()

    def product(x, at):
        high, low = split(x)
        count = x.shape[0]
        both = jnp.dot(jnp.concatenate([high, low], axis=0), li_hi[at, :], preferred_element_type=f32)
        cross = jnp.dot(high, li_lo[at, :], preferred_element_type=f32)
        return both[:count] + (both[count:] + cross)

    def solve(q):
        total = jnp.zeros((cols * rows, block), f32)
        for part, (low, count) in enumerate(cuts):
            for step in range(1, cols, 2):
                own_copy(q, part, step, came(step)).wait_recv()
            at = pl.ds(low, count)
            total = total + product(own_x[q, :, :, at].reshape(cols * rows, count), at)
        for d in range(DIRS):

            @pl.when(inside(direction_steps[d]))
            def _():
                for step in range(cols):
                    mar_copy(q, d, step, col_at(-step)).wait_recv()

        margins = jnp.concatenate([mar_x[q, d].reshape(cols * rows, LANES) for d in range(DIRS)], axis=1)
        total = total + product(margins, pl.ds(owned, DIRS * LANES))
        solved[q] = total.reshape(cols, rows, block)
        each_return(lambda d, step: ret_copy(q, d, step).start())
        for b in range(cols):
            if own_parts[b]:

                @pl.when(c == b)
                def _():
                    for step in range(1, cols):
                        sol_copy(q, b, step).start()
                    sol_in[q, b, :, pl.ds(0, own_parts[b])] = solved[q, c, :, pl.ds(0, own_parts[b])]

    def update(g, q):
        for by in range(1, subs):
            coarse_copy(q, by, sub_at(-by)).wait_recv()
        coarse = jnp.zeros((rows, LANES), f32)
        for other in range(subs):
            message = coarse_x[q, other]
            for m in range(nmodes):
                coarse = coarse + message[:, m : m + 1] * cinv_turned[pl.ds(other * nmodes + m, 1), :]
        levels = [jnp.broadcast_to(coarse[:, m : m + 1], (rows, LANES)) for m in range(nmodes)]
        for b in range(cols):
            if own_parts[b]:

                @pl.when(c != b)
                def _():
                    sol_copy(q, b, 0).wait_recv()

        for d in range(DIRS):

            @pl.when(inside(-direction_steps[d]))
            def _():
                ret_copy(q, d, 0).wait_recv()

        for t in range(tiles):
            at = pl.ds(t * LANES, LANES)
            b, offset = divmod(t * LANES, block)
            total = sol_in[q, b, :, pl.ds(offset, LANES)]
            for d in range(DIRS):
                index = jnp.broadcast_to(inverse[t, pl.ds(d, 1), :], (rows, LANES))
                total = total + jnp.where(index >= 0, lane_gather(ret_in[q, d], index & (LANES - 1)), 0.0)
            for m in range(nmodes):
                total = total + levels[m] * modes_ref[pl.ds(m, 1), at]
            lam[g, :, at] = lam[g, :, at] + damping * total

    def iteration(it, carry):
        update(0, it - 1)
        halos(0, it)
        begin(0, it)
        rest(0, it)
        forward(it)
        solve(it)
        return carry

    def start_halos():
        read_tables()
        for g in range(GROUPS):
            halos(g, g)
        load_inverse.wait()

    def split_tile(number):
        at = pl.ds(pl.multiple_of(number * LANES, LANES), LANES)
        scale = weights_ref[:, at]
        for low in range(0, block, LANES):
            high, rest_of = split((li[low : low + LANES, at] * scale).T)
            li_hi[at, low : low + LANES] = high
            li_lo[at, low : low + LANES] = rest_of

    def split_beside(number, count):
        pieces = li_hbm.shape[1] // LANES
        each = -(-pieces // count)
        for n in range(each):
            split_tile(lax.rem(number * each + n, pieces))

    weights_ref[...] = 1.0 / (1.0 + code_ref[...].astype(f32))
    build_operator(
        idx_ref, vals_ref, op_hi, op_lo, turned, low_rows, send_tables, start_halos, split_beside
    )
    begin(0, 0)
    rest(0, 0)
    forward(0)
    solve(0)
    lax.fori_loop(1, ITERS, iteration, 0)
    update(0, ITERS - 1)
    for g in range(GROUPS):
        out_ref[g * rows : (g + 1) * rows, :] = lam[g]

    def drain(q, carry):
        for d in range(DIRS):

            @pl.when(inside(-direction_steps[d]))
            def _():
                halo_copy(q, d).wait_send()
                for step in range(cols):
                    mar_copy(q, d, step, c).wait_send()

        for step in range(1, cols):
            for part in range(len(cuts)):
                own_copy(q, part, step, passed(step) if step % 2 else c).wait_send()
        for by in range(1, subs):
            coarse_copy(q, by, s).wait_send()
        each_return(lambda d, step: ret_copy(q, d, step).wait_send())
        for b in range(cols):
            if own_parts[b]:

                @pl.when(c == b)
                def _():
                    for step in range(1, cols):
                        sol_copy(q, b, step).wait_send()

        return carry

    lax.fori_loop(0, ITERS * GROUPS, drain, 0)


def local(
    subs, cols,
    adjoint_source,
    start_field,
    row_diagonal,
    row_values,
    row_columns,
    weight_code,
    slot_count,
    slot_rows,
    local_inverse,
    coarse_modes,
    coarse_inverse,
):
    ncol, owned = start_field.shape
    block, ext = local_inverse.shape
    rows = ncol // GROUPS
    rounds = ITERS * GROUPS
    vmem = pl.BlockSpec(memory_space=pltpu.VMEM)
    dma = pltpu.SemaphoreType.DMA
    return pl.pallas_call(
        functools.partial(kernel, subs, cols),
        out_shape=jax.ShapeDtypeStruct((ncol, owned), f32),
        in_specs=[vmem] * 6 + [pl.BlockSpec(memory_space=pltpu.SMEM)] + [vmem] * 3 + [pl.BlockSpec(memory_space=pl.ANY)],
        out_specs=vmem,
        scratch_shapes=[
            pltpu.VMEM((GROUPS, rows, owned), f32),
            pltpu.VMEM((1, owned), f32),
            pltpu.VMEM((rows, owned), f32),
            pltpu.VMEM((ext, owned), bf16),
            pltpu.VMEM((ext, owned), bf16),
            pltpu.VMEM((3, owned, LANES), f32),
            pltpu.VMEM((SUBLANES // (LANES // (1 << (row_values.shape[0] - 1).bit_length())), owned // SUBLANES, LANES), f32),
            pltpu.VMEM((block, ext), f32),
            pltpu.VMEM((ext, block), bf16),
            pltpu.VMEM((ext, block), bf16),
            pltpu.VMEM((1, ext), f32),
            pltpu.VMEM((SUBLANES, LANES), jnp.int32),
            pltpu.VMEM((DIRS, SUBLANES, LANES), jnp.int32),
            pltpu.VMEM((SUBLANES, LANES), jnp.int32),
            pltpu.VMEM((owned // LANES, SUBLANES, LANES), jnp.int32),
            pltpu.VMEM((LANES, coarse_inverse.shape[1]), f32),
            pltpu.VMEM((coarse_inverse.shape[1], LANES), f32),
            pltpu.VMEM((rounds, DIRS, rows, LANES), f32),
            pltpu.VMEM((rounds, DIRS, rows, LANES), f32),
            pltpu.VMEM((rounds, cols, rows, owned), f32),
            pltpu.VMEM((rounds, DIRS, rows, LANES), f32),
            pltpu.VMEM((rounds, DIRS, cols, rows, LANES), f32),
            pltpu.VMEM((rounds, subs, rows, LANES), f32),
            pltpu.VMEM((rounds, cols, rows, block), f32),
            pltpu.VMEM((rounds, cols, rows, block), f32),
            pltpu.VMEM((rounds, DIRS, rows, LANES), f32),
            dma,
            dma((DIRS,)),
            dma((DIRS,)),
            dma((rounds, DIRS)),
            dma((rounds, DIRS)),
            dma((rounds, 3, cols)),
            dma((rounds, 3, cols)),
            dma((rounds, DIRS, cols)),
            dma((rounds, DIRS, cols)),
            dma((rounds, subs)),
            dma((rounds, subs)),
            dma((rounds, cols)),
            dma((rounds, cols)),
            dma((rounds, DIRS, cols)),
            dma((rounds, DIRS)),
        ],
        compiler_params=pltpu.CompilerParams(collective_id=0, has_side_effects=True),
    )(
        adjoint_source,
        start_field,
        row_diagonal,
        row_values,
        row_columns,
        weight_code.reshape(1, ext),
        slot_count,
        slot_rows,
        coarse_modes,
        coarse_inverse,
        local_inverse,
    )


def solution(mesh):
    return jax.shard_map(
        functools.partial(local, mesh.shape["sub"], mesh.shape["col"]),
        mesh=mesh,
        in_specs=(
            P("col", "sub"),
            P("col", "sub"),
            P("sub"),
            P(None, "sub"),
            P(None, "sub"),
            P("sub"),
            P("sub", None),
            P("sub", None, None),
            P(("sub", "col"), None),
            P(None, "sub"),
            P("sub", None),
        ),
        out_specs=P("col", "sub"),
        check_vma=False,
    )
```

```python
import functools

import jax
import jax.numpy as jnp
from jax import lax
from jax.experimental import pallas as pl
from jax.experimental.pallas import tpu as pltpu
from jax.sharding import PartitionSpec as P

ITERS = 3
LANES = 128
SUBLANES = 8

direction_steps = (-2, -1, 1, 2)
damping = 0.7
highest = lax.Precision.HIGHEST
contract_last = (((1,), (1,)), ((), ()))
contract_first = (((1,), (0,)), ((), ()))
f32 = jnp.float32
bf16 = jnp.bfloat16
DIRS = len(direction_steps)
GROUPS = 1


def lane_gather(tile, low):
    return jnp.take_along_axis(tile, low, axis=1, mode="promise_in_bounds")


def split(x):
    high = x.astype(bf16)
    return high, (x - high.astype(f32)).astype(bf16)


def build_operator(idx_ref, vals_ref, op_hi, op_lo, turned, low_rows, halfway, later, beside):
    terms, owned = idx_ref.shape
    heads = op_hi.shape[0] // LANES
    tiles = owned // LANES
    width = 1 << (terms - 1).bit_length()
    per = LANES // width
    halves = SUBLANES // per
    blocks = LANES // SUBLANES
    full = (LANES, LANES)
    square_row = lax.broadcasted_iota(jnp.int32, full, 0)
    square_lane = lax.broadcasted_iota(jnp.int32, full, 1)
    eye = jnp.where(square_row == square_lane, 1.0, 0.0).astype(bf16)
    keep = [square_row % SUBLANES == square_lane // width + per * h for h in range(halves)]
    few = (blocks, LANES)
    pick = lax.broadcasted_iota(jnp.int32, few, 1) // SUBLANES == lax.broadcasted_iota(jnp.int32, few, 0)
    pick = jnp.where(pick, 1.0, 0.0).astype(bf16)

    def turn(t, carry):
        at = pl.ds(pl.multiple_of(t * LANES, LANES), LANES)
        index, value = idx_ref[:, at], vals_ref[:, at]

        def tiled(x, fill):
            x = jnp.concatenate([x, jnp.full((width - terms, LANES), fill, f32)], axis=0)
            return jnp.concatenate([x] * per, axis=0).astype(bf16)

        def turn_one(x):
            return lax.dot_general(eye, x, contract_last, preferred_element_type=f32)

        top = value.astype(bf16).astype(f32)
        turned[0, at, :] = turn_one(tiled((index >> 7).astype(f32), -1.0))
        turned[1, at, :] = turn_one(tiled(top, 0.0))
        turned[2, at, :] = turn_one(tiled(value - top, 0.0))
        low = turn_one(tiled((index & (LANES - 1)).astype(f32), -1.0))
        for h in range(halves):
            low_rows[h, pl.ds(pl.multiple_of(t * blocks, blocks), blocks), :] = lax.dot_general(
                pick, jnp.where(keep[h], low, 0.0).astype(bf16), contract_first, preferred_element_type=f32
            )
        return carry

    lax.fori_loop(0, tiles, turn, 0, unroll=tiles)

    halfway()
    lane_number = square_row.astype(f32).astype(bf16)
    tall = (heads * SUBLANES, LANES)
    head_number = (lax.broadcasted_iota(jnp.int32, tall, 0) // SUBLANES).astype(f32).astype(bf16)
    small = (SUBLANES, LANES)
    mine = [
        lax.broadcasted_iota(jnp.int32, small, 0) == lax.broadcasted_iota(jnp.int32, small, 1) // width + per * h
        for h in range(halves)
    ]
    one, zero = jnp.ones(full, bf16), jnp.zeros(full, bf16)
    none = jnp.zeros(tall, bf16)

    def repeat(x):
        pair = jnp.concatenate([x, x], axis=0).astype(bf16)
        return jnp.concatenate([pair] * (heads // 2), axis=0)

    def one_block(row):
        at = pl.ds(pl.multiple_of(row * SUBLANES, SUBLANES), SUBLANES)
        head = turned[0, at, :]
        value_hi, value_lo = repeat(turned[1, at, :]), repeat(turned[2, at, :])
        left_hi, left_lo, right = [], [], []
        for h in range(halves):
            hit = repeat(jnp.where(mine[h], head, -1.0)) == head_number
            left_hi.append(jnp.where(hit, value_hi, none))
            left_lo.append(jnp.where(hit, value_lo, none))
            low = jnp.broadcast_to(low_rows[h, pl.ds(row, 1), :], (2 * SUBLANES, LANES)).astype(bf16)
            low = jnp.concatenate([low] * (LANES // (2 * SUBLANES)), axis=0)
            right.append(jnp.where(low == lane_number, one, zero))
        left = jnp.concatenate([jnp.concatenate(left_hi, axis=1), jnp.concatenate(left_lo, axis=1)], axis=0)
        out = lax.dot_general(left, jnp.concatenate(right, axis=1), contract_last, preferred_element_type=f32)
        return out[: heads * SUBLANES] + out[heads * SUBLANES :]

    def one_tile(t, carry):
        at = pl.ds(pl.multiple_of(t * LANES, LANES), LANES)
        outs = [one_block(t * blocks + b) for b in range(blocks)]
        for h in range(heads):
            x = jnp.concatenate([out[h * SUBLANES : (h + 1) * SUBLANES] for out in outs], axis=0).T
            high, low = split(x)
            op_hi[h * LANES : (h + 1) * LANES, at] = high
            op_lo[h * LANES : (h + 1) * LANES, at] = low
        return carry

    early = tiles // 4 * 2
    lax.fori_loop(0, early, one_tile, 0, unroll=6)
    later()

    def one_tile_beside(t, carry):
        beside(t - early, tiles - early)
        return one_tile(t, carry)

    lax.fori_loop(early, tiles, one_tile_beside, 0, unroll=6)


def kernel(
    subs, cols,
    source_ref, start_ref, diag_ref, vals_ref, idx_ref, code_ref, count_ref, rows_ref, modes_ref, cinv_ref, li_hbm,
    out_ref,
    lam, diag, base, op_hi, op_lo, turned, low_rows, li, li_hi, li_lo, weights_ref, table, tables, fidx, inverse, cinv_pad, cinv_turned,
    halo_out, halo_in, own_x, mar_out, mar_x, coarse_x, solved, sol_in, ret_in,
    li_sem, tab_s, tab_r, halo_s, halo_r, own_s, own_r, mar_s, mar_r, co_s, co_r, sol_s, sol_r, ret_s, ret_r,
):
    s = lax.axis_index("sub")
    c = lax.axis_index("col")
    owned = start_ref.shape[1]
    rows = lam.shape[1]
    tiles = owned // LANES
    block = li_hbm.shape[0]
    nmodes = modes_ref.shape[0]
    pieces = 3
    edges = [tiles * n // pieces * LANES for n in range(pieces + 1)]
    cuts = tuple((low, high - low) for low, high in zip(edges, edges[1:]))

    def sub_at(by):
        return lax.rem(s + (by + subs), subs)

    def col_at(by):
        return lax.rem(c + (by + cols), cols)

    def inside(by):
        return jnp.logical_and(s + by >= 0, s + by < subs)

    def remote(src, dst, send, recv, where):
        return pltpu.make_async_remote_copy(
            src_ref=src, dst_ref=dst, send_sem=send, recv_sem=recv,
            device_id=where, device_id_type=pl.DeviceIdType.MESH,
        )

    load_inverse = pltpu.make_async_copy(li_hbm, li, li_sem)
    load_inverse.start()

    partners = []
    for step in range(1, cols):
        partners.append((0, step))
    for by in range(1, subs):
        near = by in (1, 2, subs - 1, subs - 2)
        for step in range(cols if near else 1):
            partners.append((by, step))
    barrier = pltpu.get_barrier_semaphore()
    tables[...] = jnp.full(tables.shape, -1, jnp.int32)
    for clean in (halo_in, mar_x, ret_in, coarse_x):
        clean[...] = jnp.zeros_like(clean)
    for by, step in partners:
        pl.semaphore_signal(
            barrier, inc=1, device_id=(sub_at(by), col_at(step)), device_id_type=pl.DeviceIdType.MESH
        )
    lane = lax.broadcasted_iota(jnp.int32, (1, LANES), 1)
    for d in range(DIRS):
        table[pl.ds(d, 1), :] = jnp.where(lane < count_ref[0, d], rows_ref[0, pl.ds(d, 1), :], -1)
    for t in range(tiles):
        diag[:, t * LANES : (t + 1) * LANES] = diag_ref[pl.ds(t * LANES, LANES)].reshape(1, LANES)
    for g in range(GROUPS):
        lam[g] = start_ref[g * rows : (g + 1) * rows, :]
    members = subs * nmodes
    cinv_pad[...] = jnp.zeros_like(cinv_pad)
    cinv_pad[pl.ds(0, nmodes), :] = cinv_ref[...]
    square = (members, members)
    same = lax.broadcasted_iota(jnp.int32, square, 0) == lax.broadcasted_iota(jnp.int32, square, 1)
    cinv_turned[...] = lax.dot_general(
        jnp.where(same, 1.0, 0.0), cinv_pad[...], contract_last, precision=highest, preferred_element_type=f32
    )

    def tab_copy(d):
        return remote(table, tables.at[d], tab_s.at[d], tab_r.at[d], (sub_at(direction_steps[d]), c))

    def send_tables():
        pl.semaphore_wait(barrier, len(partners))
        for d in range(DIRS):

            @pl.when(inside(direction_steps[d]))
            def _():
                tab_copy(d).start()

    def read_tables():
        for d in range(DIRS):

            @pl.when(inside(direction_steps[d]))
            def _():
                tab_copy(d).wait_send()

            @pl.when(inside(-direction_steps[d]))
            def _():
                tab_copy(d).wait_recv()

        for d in range(DIRS):
            fidx[pl.ds(d, 1), :] = tables[d, pl.ds(d, 1), :]

        slot_number = lax.broadcasted_iota(jnp.int32, (LANES, LANES), 0).astype(f32) + 1.0
        lane_full = lax.broadcasted_iota(jnp.int32, (LANES, LANES), 1).astype(f32)
        for d in range(DIRS):
            wanted = jnp.broadcast_to(fidx[pl.ds(d, 1), :].astype(f32), (LANES, LANES)).T

            def invert(number, carry):
                hit = wanted == lane_full + lax.convert_element_type(number * LANES, f32)
                found = jnp.sum(jnp.where(hit, slot_number, 0.0), axis=0, keepdims=True)
                inverse[number, pl.ds(d, 1), :] = found.astype(jnp.int32) - 1
                return carry

            lax.fori_loop(0, tiles, invert, 0, unroll=4)

    def pack(read_tile, put):
        for d in range(DIRS):
            index = jnp.broadcast_to(fidx[pl.ds(d, 1), :], (rows, LANES))
            low, high = index & (LANES - 1), index >> 7
            total = jnp.zeros((rows, LANES), f32)
            for t in range(tiles):
                total = jnp.where(high == t, lane_gather(read_tile(t), low), total)
            put(d, total)

    def operate(x, low, high, at):
        count = x.shape[0]
        top, bottom = split(x)
        stretch = pl.ds(low, high - low)
        both = jnp.dot(jnp.concatenate([top, bottom], axis=0), op_hi[stretch, at], preferred_element_type=f32)
        cross = jnp.dot(top, op_lo[stretch, at], preferred_element_type=f32)
        return both[:count] + (both[count:] + cross)

    own_parts = [max(0, min((b + 1) * block, owned) - b * block) for b in range(cols)]
    slot_homes = [divmod(owned + d * LANES, block) for d in range(DIRS)]

    def halo_copy(q, d):
        return remote(
            halo_out.at[q, d], halo_in.at[q, d], halo_s.at[q, d], halo_r.at[q, d], (sub_at(-direction_steps[d]), c)
        )

    sibling = c + 1 - 2 * lax.rem(c, 2)

    def own_copy(q, part, step, slot):
        piece = own_x.at[q, slot, :, pl.ds(*cuts[part])]
        where = sibling if step % 2 else col_at(step)
        return remote(piece, piece, own_s.at[q, part, step], own_r.at[q, part, step], (s, where))

    def passed(step):
        return c if step == 1 else col_at(1 - step)

    def came(step):
        return lax.rem(sibling + (1 - step + cols), cols) if step % 2 else col_at(-step)

    def forward(q):
        for part in range(len(cuts)):
            for step in range(2, cols, 2):
                own_copy(q, part, step, came(step)).wait_recv()
                own_copy(q, part, step + 1, passed(step + 1)).start()

    def mar_copy(q, d, step, slot):
        return remote(
            mar_out.at[q, d], mar_x.at[q, d, slot], mar_s.at[q, d, step], mar_r.at[q, d, step],
            (sub_at(-direction_steps[d]), col_at(step)),
        )

    def coarse_copy(q, by, slot):
        return remote(coarse_x.at[q, slot], coarse_x.at[q, slot], co_s.at[q, by], co_r.at[q, by], (sub_at(by), c))

    def sol_copy(q, b, step):
        width = own_parts[b]
        return remote(
            solved.at[q, col_at(step), :, pl.ds(0, width)], sol_in.at[q, b, :, pl.ds(0, width)],
            sol_s.at[q, step], sol_r.at[q, b], (s, col_at(step)),
        )

    def ret_copy(q, d, step):
        return remote(
            solved.at[q, col_at(step), :, pl.ds(slot_homes[d][1], LANES)], ret_in.at[q, d],
            ret_s.at[q, d, step], ret_r.at[q, d], (sub_at(direction_steps[d]), col_at(step)),
        )

    def each_return(act):
        for d in range(DIRS):

            @pl.when(jnp.logical_and(c == slot_homes[d][0], inside(direction_steps[d])))
            def _():
                for step in range(cols):
                    act(d, step)

    def halos(g, q):
        def put_halo(d, total):
            halo_out[q, d] = total

            @pl.when(inside(-direction_steps[d]))
            def _():
                halo_copy(q, d).start()

        pack(lambda t: lam[g, :, t * LANES : (t + 1) * LANES], put_halo)

    def begin(g, q):
        for low, count in cuts:
            at = pl.ds(low, count)
            held = lam[g, :, at]
            base[:, at] = source_ref[g * rows : (g + 1) * rows, at] - diag[:, at] * held - operate(lam[g], 0, owned, at)

    def rest(g, q):
        for d in range(DIRS):

            @pl.when(inside(direction_steps[d]))
            def _():
                halo_copy(q, d).wait_recv()

        slots = jnp.concatenate([halo_in[q, d] for d in range(DIRS)], axis=1)
        for part, (low, count) in enumerate(cuts):
            at = pl.ds(low, count)
            own_x[q, c, :, at] = base[:, at] - operate(slots, owned, owned + DIRS * LANES, at)
            for step in [*range(2, cols, 2), 1]:
                own_copy(q, part, step, c).start()

        def put_margin(d, total):
            mar_out[q, d] = total

            @pl.when(inside(-direction_steps[d]))
            def _():
                for step in range(cols):
                    mar_copy(q, d, step, c).start()

        pack(lambda t: own_x[q, c, :, t * LANES : (t + 1) * LANES], put_margin)
        message = jnp.zeros((rows, LANES), f32)
        for m in range(nmodes):
            part = jnp.zeros((rows, LANES), f32)
            for t in range(tiles):
                at = pl.ds(t * LANES, LANES)
                part = part + own_x[q, c, :, at] * modes_ref[pl.ds(m, 1), at]
            message = jnp.where(lane == m, jnp.sum(part, axis=1, keepdims=True), message)
        coarse_x[q, s] = message
        for by in range(1, subs):
            coarse_copy(q, by, s).start()

    def product(x, at):
        high, low = split(x)
        count = x.shape[0]
        both = jnp.dot(jnp.concatenate([high, low], axis=0), li_hi[at, :], preferred_element_type=f32)
        cross = jnp.dot(high, li_lo[at, :], preferred_element_type=f32)
        return both[:count] + (both[count:] + cross)

    def solve(q):
        total = jnp.zeros((cols * rows, block), f32)
        for part, (low, count) in enumerate(cuts):
            for step in range(1, cols, 2):
                own_copy(q, part, step, came(step)).wait_recv()
            at = pl.ds(low, count)
            total = total + product(own_x[q, :, :, at].reshape(cols * rows, count), at)
        for d in range(DIRS):

            @pl.when(inside(direction_steps[d]))
            def _():
                for step in range(cols):
                    mar_copy(q, d, step, col_at(-step)).wait_recv()

        margins = jnp.concatenate([mar_x[q, d].reshape(cols * rows, LANES) for d in range(DIRS)], axis=1)
        total = total + product(margins, pl.ds(owned, DIRS * LANES))
        solved[q] = total.reshape(cols, rows, block)
        each_return(lambda d, step: ret_copy(q, d, step).start())
        for b in range(cols):
            if own_parts[b]:

                @pl.when(c == b)
                def _():
                    for step in range(1, cols):
                        sol_copy(q, b, step).start()
                    sol_in[q, b, :, pl.ds(0, own_parts[b])] = solved[q, c, :, pl.ds(0, own_parts[b])]

    def update(g, q):
        for by in range(1, subs):
            coarse_copy(q, by, sub_at(-by)).wait_recv()
        coarse = jnp.zeros((rows, LANES), f32)
        for other in range(subs):
            message = coarse_x[q, other]
            for m in range(nmodes):
                coarse = coarse + message[:, m : m + 1] * cinv_turned[pl.ds(other * nmodes + m, 1), :]
        levels = [jnp.broadcast_to(coarse[:, m : m + 1], (rows, LANES)) for m in range(nmodes)]
        for b in range(cols):
            if own_parts[b]:

                @pl.when(c != b)
                def _():
                    sol_copy(q, b, 0).wait_recv()

        for d in range(DIRS):

            @pl.when(inside(-direction_steps[d]))
            def _():
                ret_copy(q, d, 0).wait_recv()

        for t in range(tiles):
            at = pl.ds(t * LANES, LANES)
            b, offset = divmod(t * LANES, block)
            total = sol_in[q, b, :, pl.ds(offset, LANES)]
            for d in range(DIRS):
                index = jnp.broadcast_to(inverse[t, pl.ds(d, 1), :], (rows, LANES))
                total = total + jnp.where(index >= 0, lane_gather(ret_in[q, d], index & (LANES - 1)), 0.0)
            for m in range(nmodes):
                total = total + levels[m] * modes_ref[pl.ds(m, 1), at]
            lam[g, :, at] = lam[g, :, at] + damping * total

    def iteration(it, carry):
        update(0, it - 1)
        halos(0, it)
        begin(0, it)
        rest(0, it)
        forward(it)
        solve(it)
        return carry

    def start_halos():
        read_tables()
        for g in range(GROUPS):
            halos(g, g)
        load_inverse.wait()

    def split_tile(number):
        at = pl.ds(pl.multiple_of(number * LANES, LANES), LANES)
        scale = weights_ref[:, at]
        for low in range(0, block, LANES):
            high, rest_of = split((li[low : low + LANES, at] * scale).T)
            li_hi[at, low : low + LANES] = high
            li_lo[at, low : low + LANES] = rest_of

    def split_beside(number, count):
        pieces = li_hbm.shape[1] // LANES
        each = -(-pieces // count)
        for n in range(each):
            split_tile(lax.rem(number * each + n, pieces))

    weights_ref[...] = 1.0 / (1.0 + code_ref[...].astype(f32))
    build_operator(
        idx_ref, vals_ref, op_hi, op_lo, turned, low_rows, send_tables, start_halos, split_beside
    )
    begin(0, 0)
    rest(0, 0)
    forward(0)
    solve(0)
    lax.fori_loop(1, ITERS, iteration, 0)
    update(0, ITERS - 1)
    for g in range(GROUPS):
        out_ref[g * rows : (g + 1) * rows, :] = lam[g]

    def drain(q, carry):
        for d in range(DIRS):

            @pl.when(inside(-direction_steps[d]))
            def _():
                halo_copy(q, d).wait_send()
                for step in range(cols):
                    mar_copy(q, d, step, c).wait_send()

        for step in range(1, cols):
            for part in range(len(cuts)):
                own_copy(q, part, step, passed(step) if step % 2 else c).wait_send()
        for by in range(1, subs):
            coarse_copy(q, by, s).wait_send()
        each_return(lambda d, step: ret_copy(q, d, step).wait_send())
        for b in range(cols):
            if own_parts[b]:

                @pl.when(c == b)
                def _():
                    for step in range(1, cols):
                        sol_copy(q, b, step).wait_send()

        return carry

    lax.fori_loop(0, ITERS * GROUPS, drain, 0)


def local(
    subs, cols,
    adjoint_source,
    start_field,
    row_diagonal,
    row_values,
    row_columns,
    weight_code,
    slot_count,
    slot_rows,
    local_inverse,
    coarse_modes,
    coarse_inverse,
):
    ncol, owned = start_field.shape
    block, ext = local_inverse.shape
    rows = ncol // GROUPS
    rounds = ITERS * GROUPS
    vmem = pl.BlockSpec(memory_space=pltpu.VMEM)
    dma = pltpu.SemaphoreType.DMA
    return pl.pallas_call(
        functools.partial(kernel, subs, cols),
        out_shape=jax.ShapeDtypeStruct((ncol, owned), f32),
        in_specs=[vmem] * 6 + [pl.BlockSpec(memory_space=pltpu.SMEM)] + [vmem] * 3 + [pl.BlockSpec(memory_space=pl.ANY)],
        out_specs=vmem,
        scratch_shapes=[
            pltpu.VMEM((GROUPS, rows, owned), f32),
            pltpu.VMEM((1, owned), f32),
            pltpu.VMEM((rows, owned), f32),
            pltpu.VMEM((ext, owned), bf16),
            pltpu.VMEM((ext, owned), bf16),
            pltpu.VMEM((3, owned, LANES), f32),
            pltpu.VMEM((SUBLANES // (LANES // (1 << (row_values.shape[0] - 1).bit_length())), owned // SUBLANES, LANES), f32),
            pltpu.VMEM((block, ext), f32),
            pltpu.VMEM((ext, block), bf16),
            pltpu.VMEM((ext, block), bf16),
            pltpu.VMEM((1, ext), f32),
            pltpu.VMEM((SUBLANES, LANES), jnp.int32),
            pltpu.VMEM((DIRS, SUBLANES, LANES), jnp.int32),
            pltpu.VMEM((SUBLANES, LANES), jnp.int32),
            pltpu.VMEM((owned // LANES, SUBLANES, LANES), jnp.int32),
            pltpu.VMEM((LANES, coarse_inverse.shape[1]), f32),
            pltpu.VMEM((coarse_inverse.shape[1], LANES), f32),
            pltpu.VMEM((rounds, DIRS, rows, LANES), f32),
            pltpu.VMEM((rounds, DIRS, rows, LANES), f32),
            pltpu.VMEM((rounds, cols, rows, owned), f32),
            pltpu.VMEM((rounds, DIRS, rows, LANES), f32),
            pltpu.VMEM((rounds, DIRS, cols, rows, LANES), f32),
            pltpu.VMEM((rounds, subs, rows, LANES), f32),
            pltpu.VMEM((rounds, cols, rows, block), f32),
            pltpu.VMEM((rounds, cols, rows, block), f32),
            pltpu.VMEM((rounds, DIRS, rows, LANES), f32),
            dma,
            dma((DIRS,)),
            dma((DIRS,)),
            dma((rounds, DIRS)),
            dma((rounds, DIRS)),
            dma((rounds, 3, cols)),
            dma((rounds, 3, cols)),
            dma((rounds, DIRS, cols)),
            dma((rounds, DIRS, cols)),
            dma((rounds, subs)),
            dma((rounds, subs)),
            dma((rounds, cols)),
            dma((rounds, cols)),
            dma((rounds, DIRS, cols)),
            dma((rounds, DIRS)),
        ],
        compiler_params=pltpu.CompilerParams(collective_id=0, has_side_effects=True),
    )(
        adjoint_source,
        start_field,
        row_diagonal,
        row_values,
        row_columns,
        weight_code.reshape(1, ext),
        slot_count,
        slot_rows,
        coarse_modes,
        coarse_inverse,
        local_inverse,
    )


def solution(mesh):
    return jax.shard_map(
        functools.partial(local, mesh.shape["sub"], mesh.shape["col"]),
        mesh=mesh,
        in_specs=(
            P("col", "sub"),
            P("col", "sub"),
            P("sub"),
            P(None, "sub"),
            P(None, "sub"),
            P("sub"),
            P("sub", None),
            P("sub", None, None),
            P(("sub", "col"), None),
            P(None, "sub"),
            P("sub", None),
        ),
        out_specs=P("col", "sub"),
        check_vma=False,
    )
```
